256 devices in a mesh: row: 32 (over x, z_hi, core), col: 8 (over y, z_lo).
Axes of the slice: x: 4, y: 4, z: 8 (z_hi: 4, z_lo: 2; z = z_hi * 2 + z_lo), core: 2. Of those that a mesh axis runs over, the one named last changes fastest.
Arguments:
- sigma_anc: float32 [128, 128, 128, 128], P('row', 'col'), as said below
- panel: float32 [2, 128, 128, 512], P(None, 'row'), may hold values from -0.12 to 0.12
- pattern: int32 [2, 64], replicated, may hold values from 0 to 127, as said below
- linv: float32 [2, 512, 512], replicated, as said below
Outputs:
- sigma_sj: float32 [2, 128, 128, 512], P(None, 'row')
- sigma_jj: float32 [2, 512, 512], replicated
The draws below stay inside these ranges and needn't reach their ends.
Inputs may be any that keep to these rules, and one draw needn't show every extreme that they name: `pattern`: each row lists 64 distinct ancestor block indices in increasing order; 0 and 127 are always among them. `sigma_anc`: symmetric as a matrix of order 128 * 128 in ancestor order. `linv`: lower triangular, diagonal entries between 1 and 2.
All inputs are finite; a program needn't handle non-finite values.
Results may differ from the reference program's by a relative error of at most 0.0001.
Values sent between devices are 32-bit elements; how exact they have to be, the bound alone decides.
A program may use at most 128 MiB of HBM per device.

```python
import jax
import jax.numpy as jnp
from jax import lax

W = 512
BS = 128
SUPER = 2
QR = 4
NB = 128
QC = 16
KS = 64
N_ROW = 32
N_COL = 8


def draw_sigma_anc(key, part):
    first, second = jax.random.split(key, 2)
    order = NB * BS
    base = jax.random.normal(first, (NB, NB, BS, BS), jnp.float32)
    full = (base + jnp.transpose(base, (1, 0, 3, 2))) * (1.4142135 / jnp.sqrt(jnp.float32(order)))
    diag_values = jax.random.uniform(second, (NB, BS), jnp.float32, 1.0, 4.0)
    block_eye = jnp.eye(NB, dtype=jnp.float32)[:, :, None, None]
    inner_eye = jnp.eye(BS, dtype=jnp.float32)[None, None, :, :]
    full = full + block_eye * inner_eye * diag_values[:, None, :, None]
    storage = jnp.arange(NB, dtype=jnp.int32)
    row_map = storage % QR * N_ROW + storage // QR
    col_map = storage % QC * N_COL + storage // QC
    return full[row_map][:, col_map]


def draw_pattern(key, part):
    keys = jax.random.split(key, SUPER)

    def single(one_key):
        inner = (jax.random.permutation(one_key, NB - 2)[:KS - 2] + 1).astype(jnp.int32)
        ends = jnp.array([0, NB - 1], dtype=jnp.int32)
        return jnp.sort(jnp.concatenate([ends, inner]))
    return jax.vmap(single)(keys).astype(jnp.int32)


def draw_linv(key, part):
    first, second = jax.random.split(key)
    lower = jax.random.normal(first, (SUPER, W, W), jnp.float32) / jnp.sqrt(jnp.float32(W))
    diagonal = jax.random.uniform(second, (SUPER, W), jnp.float32, 1.0, 2.0)
    return jnp.tril(lower, -1) + diagonal[:, :, None] * jnp.eye(W, dtype=jnp.float32)[None]


def level_of(rng, shape, shards, low, top_value):
    level, own = 1.0, jax.random.fold_in(rng, 6)
    for dim, shards_of in shards:
        steps = jnp.exp(jax.random.uniform(jax.random.fold_in(own, dim), (shards_of,), jnp.float32, low / len(shards), top_value / len(shards)))
        level = level * jnp.repeat(steps, shape[dim] // shards_of).reshape([-1 if axis == dim else 1 for axis in range(len(shape))])
    return level


def normal_values(own_key, shape, width, bound, pieces=(), kind=jnp.bfloat16):
    result = width * jax.random.normal(own_key, shape, jnp.float32)
    if pieces:
        result = result * level_of(own_key, shape, pieces, -0.22, 0.18)
    return jnp.clip(result, -bound, bound).astype(kind)


def setup_inputs(seed: int = 0) -> dict:
    arg_keys = jax.random.split(jax.random.key(seed), 5)
    return {
        "sigma_anc": draw_sigma_anc(jax.random.fold_in(arg_keys[4], 71), 0),
        "panel": normal_values(arg_keys[1], (SUPER, NB, BS, W), 0.02, 0.12, ((1, 32),), jnp.float32),
        "pattern": draw_pattern(jax.random.fold_in(arg_keys[4], 71), 0),
        "linv": draw_linv(jax.random.fold_in(arg_keys[4], 71), 0),
    }


def reference(sigma_anc, panel, pattern, linv):
    highest = lax.Precision.HIGHEST
    sj_list = []
    jj_list = []
    for number in range(SUPER):
        blocks = pattern[number].astype(jnp.int32)
        store_rows = ((blocks % N_ROW) * QR + blocks // N_ROW).astype(jnp.int32)
        store_cols = ((blocks % N_COL) * QC + blocks // N_COL).astype(jnp.int32)
        picked = sigma_anc[store_rows][:, store_cols]
        dense = jnp.transpose(picked, (0, 2, 1, 3)).reshape(KS * BS, KS * BS)
        factor = panel[number][store_rows].reshape(KS * BS, W)
        updated = jnp.dot(factor, linv[number], precision=highest, preferred_element_type=jnp.float32)
        product = jnp.dot(dense, updated, precision=highest, preferred_element_type=jnp.float32)
        placed = jnp.zeros((NB, BS, W), jnp.float32).at[store_rows].set(-product.reshape(KS, BS, W))
        inner = jnp.dot(linv[number].T, linv[number], precision=highest, preferred_element_type=jnp.float32)
        inner = inner + jnp.dot(updated.T, product, precision=highest, preferred_element_type=jnp.float32)
        sj_list.append(placed)
        jj_list.append(inner)
    return jnp.stack(sj_list), jnp.stack(jj_list)
```

```python
import jax
import jax.numpy as jnp
from jax import lax
from jax.experimental import pallas as pl
from jax.experimental.pallas import tpu as pltpu
from jax.sharding import PartitionSpec as P

MESH = pl.DeviceIdType.MESH
BF = jnp.bfloat16
F32 = jnp.float32
CH = 4
ORDER = (
    ("p", 0), ("o", 0), ("o", 1), ("p", 1), ("p", 2), ("b", 0), ("o", 2), ("b", 1),
    ("o", 3), ("p", 3), ("v", 0), ("c", 0), ("b", 2), ("d", 0), ("c", 1), ("e", 0),
    ("b", 3), ("d", 1), ("m", 0), ("f", 0), ("g", 0), ("h", 0), ("c", 2), ("i", 0),
    ("e", 1), ("d", 2), ("m", 1), ("k", 0), ("f", 1), ("j", 0), ("g", 1), ("c", 3),
    ("h", 1), ("i", 1), ("d", 3), ("e", 2), ("m", 2), ("f", 2), ("g", 2), ("h", 2),
    ("k", 1), ("j", 1), ("e", 3), ("i", 2), ("m", 3), ("f", 3), ("g", 3), ("h", 3),
    ("k", 2), ("j", 2), ("i", 3), ("k", 3), ("j", 3), ("l", 0), ("l", 1), ("l", 2),
    ("l", 3),
)
NN = (((1,), (0,)), ((), ()))


def split(v):
    hi = v.astype(BF)
    return hi, (v - hi.astype(F32)).astype(BF)


def dot3(a, b, dims=NN):
    dot = lambda p, q: lax.dot_general(p, q, dims, preferred_element_type=F32)
    return dot(a[0], b[0]) + (dot(a[0], b[1]) + dot(a[1], b[0]))


def kernel(
    s_ref, panel_ref, linv_ref, mask_ref, sj_ref, jj_ref,
    so, sp, scat, uto, uts, utp, ucat, gu, bs,
    tt, ol, nl, yl, zl_, yts, yf, gs, gx, gz, gzl,
    s_loc, s_s, s_r, u_s, u_r, o_s, o_r, n_s, n_r, y_s, y_r, z_s, z_r,
    a_s, a_r, b_s, b_r, gx_s, gx_r, gz_s, gz_r, ga_s, ga_r, gb_s, gb_r, gc_s, gc_r, gd_s, gd_r,
):
    row = lax.axis_index("row")
    col = lax.axis_index("col")
    x, zh, k = row // 8, (row // 2) % 4, row % 2
    y, zl = col // 2, col % 2
    z = zh * 2 + zl
    other = 1 - k

    def dev(x, y, zh, zl, k):
        return ((x * 4 + zh) * 2 + k, y * 2 + zl)

    def at_x(d):
        return dev((x + d) % 4, y, zh, zl, k)

    def at_y(d):
        return dev(x, (y + d) % 4, zh, zl, k)

    def at_zh(d):
        return dev(x, y, (zh + d) % 4, zl, k)

    def at_z(d):
        t = (z + d) % 8
        return dev(x, y, t // 2, t % 2, k)

    partner = dev(x, y, zh, zl, other)
    cross = dev(x, y, zh, 1 - zl, other)
    peers = [partner, cross]
    peers += [at_x(d) for d in (1, 2, 3)] + [at_y(d) for d in (1, 2, 3)] + [at_z(d) for d in range(1, 8)]

    sent = []

    def remote(src, dst, send, recv, device):
        return pltpu.make_async_remote_copy(
            src_ref=src, dst_ref=dst, send_sem=send, recv_sem=recv, device_id=device, device_id_type=MESH
        )

    def push(src, dst, send, recv, device):
        copy = remote(src, dst, send, recv, device)
        copy.start()
        sent.append(copy)

    def arrived(dst, send, recv):
        remote(dst, dst, send, recv, partner).wait_recv()

    barrier = pltpu.get_barrier_semaphore()
    for peer in peers:
        pl.semaphore_signal(barrier, inc=1, device_id=peer, device_id_type=MESH)

    offs = (2, 1, 3, 0)
    local = []
    for p in range(4):
        copy = pltpu.make_async_copy(s_ref.at[:, :, (x + offs[p]) % 4], so.at[p], s_loc.at[p])
        copy.start()
        local.append(copy)

    def update(j):
        a = split(panel_ref[j])
        b = split(linv_ref[j])
        return dot3(a, b).T * mask_ref[j, 0:1, :]

    uts[...] = update(other)
    pl.semaphore_wait(barrier, len(peers))
    push(uts, utp, u_s.at[0], u_r.at[0], partner)
    for p in range(4):
        push(s_ref.at[:, :, (x + offs[p]) % 4], sp.at[p], s_s.at[p], s_r.at[p], partner)
    ut = update(k)
    uto[...] = ut
    ucat[:, 0:512], ucat[:, 1024:1536] = split(ut)

    def spread(p, half, src):
        def body(i, carry):
            r = pl.multiple_of(half * 512 + i * 128, 128)
            for m in range(4):
                hi, lo = split(src[p, i, m])
                scat[p, pl.ds(r, 128), m * 128 : (m + 1) * 128] = lo
                scat[p, pl.ds(1024 + r, 128), m * 128 : (m + 1) * 128] = hi
            return carry

        lax.fori_loop(0, 4, body, 0)

    def phase_p(p):
        local[p].wait()
        spread(p, 0, so)
        if p == 0:
            arrived(utp, u_s.at[0], u_r.at[0])
            ucat[:, 512:1024], ucat[:, 1536:2048] = split(utp[...])
        arrived(sp.at[p], s_s.at[p], s_r.at[p])
        spread(p, 1, sp)
        dot = lambda a, b: jnp.dot(a, b, preferred_element_type=F32)
        tt[p] = dot(ucat[...], scat[p]) + dot(ucat[:, 0:1024], scat[p, 1024:2048])

    def phase_o(t):
        r = t * 128
        push(tt.at[0, r : r + 64], ol.at[t, 0], o_s.at[t, 0], o_r.at[t, 0], at_x(1))
        push(tt.at[0, r + 64 : r + 128], ol.at[t, 1], o_s.at[t, 1], o_r.at[t, 1], at_x(3))

    def phase_v(t):
        @pl.when(k == zl)
        def _():
            gu[0], gu[1] = split(uto[...].T)

        @pl.when(k != zl)
        def _():
            gu[0], gu[1] = split(utp[...].T)

        uto[...] = linv_ref[k].T
        first = jnp.where((x == 0) & (z == 0), 1.0, 0.0).astype(F32)
        rows = [uto[pl.ds(pl.multiple_of(t * 128 + y * 32, 32), 32)] for t in range(CH)]
        base = dot3(split(jnp.concatenate(rows)), split(linv_ref[k])) * first
        for t in range(CH):
            bs[t] = base[t * 32 : t * 32 + 32]

    def phase_b(t):
        for s in (0, 1):
            arrived(ol.at[t, s], o_s.at[t, s], o_r.at[t, s])
            r = slice(t * 128 + s * 64, t * 128 + s * 64 + 64)
            tt[1 + s, r] = tt[1 + s, r] + ol[t, s]
            push(tt.at[1 + s, t * 128 : t * 128 + 128], nl.at[t, s], n_s.at[t, s], n_r.at[t, s], at_x(1 + 2 * s))

    def phase_c(t):
        for s in (0, 1):
            arrived(nl.at[t, s], n_s.at[t, s], n_r.at[t, s])
        r = slice(t * 128, t * 128 + 128)
        tt[3, r] = tt[3, r] + (nl[t, 0] + nl[t, 1])
        for d in (1, 2, 3):
            q = (y + d) % 4
            push(tt.at[3, pl.ds(pl.multiple_of(t * 128 + q * 32, 32), 32)], yl.at[t, y], y_s.at[t, d], y_r.at[t, y], at_y(d))
        yl[t, y] = tt[3, pl.ds(pl.multiple_of(t * 128 + y * 32, 32), 32)]

    def phase_d(t):
        for d in (1, 2, 3):
            q = (y + d) % 4
            arrived(yl.at[t, q], y_s.at[t, d], y_r.at[t, q])
        for d in (1, 2, 3):
            q = (zh + d) % 4
            push(yl.at[t, q], zl_.at[t, zh], z_s.at[t, d], z_r.at[t, zh], at_zh(d))

    def phase_e(t):
        yt = yl[t, zh]
        for d in (1, 2, 3):
            q = (zh + d) % 4
            arrived(zl_.at[t, q], z_s.at[t, d], z_r.at[t, q])
            yt = yt + zl_[t, q]
        yts[t] = yt

        @pl.when(k == zl)
        def _():
            yf[t, y, k] = yt

        @pl.when(k != zl)
        def _():
            remote(yts.at[t], yf.at[t, y, k], a_s.at[t, 0], a_r.at[t, k], partner).start()

        push(yts.at[t], yf.at[t, y, k], a_s.at[t, 1], a_r.at[t, k], dev(x, y, zh, 1 - zl, zl))
        yh, yl_ = split(yt)
        g = jnp.dot(jnp.concatenate([yh, yl_]), gu[0], preferred_element_type=F32)
        g2 = jnp.dot(yh, gu[1], preferred_element_type=F32)
        gs[t] = (g[0:32] + bs[t]) + (g[32:64] + g2)
        for d in (1, 2, 3):
            q = (x + d) % 4
            push(gs.at[t, pl.ds(pl.multiple_of(q * 8, 8), 8)], gx.at[t, x], gx_s.at[t, d], gx_r.at[t, x], at_x(d))

    def phase_f(t):
        arrived(yf.at[t, y, other], a_s.at[t, 0], a_r.at[t, other])

        @pl.when(k != zl)
        def _():
            arrived(yf.at[t, y, k], a_s.at[t, 0], a_r.at[t, k])

        for d in (1, 2, 3):
            push(yf.at[t, y], yf.at[t, y], b_s.at[t, d], b_r.at[t, y], at_y(d))
    def phase_m(t):
        g = gs[t, pl.ds(pl.multiple_of(x * 8, 8), 8)]
        for d in (1, 2, 3):
            q = (x + d) % 4
            arrived(gx.at[t, q], gx_s.at[t, d], gx_r.at[t, q])
            g = g + gx[t, q]
        for q in range(4):
            gz[t, q] = g[:, q * 128 : (q + 1) * 128]
        for d in range(1, 8):
            q = (z + d) % 8
            push(gz.at[t, q // 2], gzl.at[t, z], gz_s.at[t, d], gz_r.at[t, z], at_z(d))

    def tile_row(t, x, y):
        return pl.multiple_of(t * 128 + y * 32 + x * 8, 8)

    def phase_g(t):
        g = gz[t, zh]
        for d in range(1, 8):
            q = (z + d) % 8
            arrived(gzl.at[t, q], gz_s.at[t, d], gz_r.at[t, q])
            g = g + gzl[t, q]
        r = pl.ds(tile_row(t, x, y), 8)
        c = pl.ds(pl.multiple_of(zh * 128, 128), 128)
        jj_ref[k, r, c] = g
        for d in (1, 2, 3):
            push(jj_ref.at[k, r, c], jj_ref.at[k, r, c], ga_s.at[t, d], ga_r.at[t, zh], at_zh(d))

    def phase_h(t):
        r = pl.ds(tile_row(t, x, y), 8)
        for d in (1, 2, 3):
            q = (zh + d) % 4
            c = pl.ds(pl.multiple_of(q * 128, 128), 128)
            arrived(jj_ref.at[k, r, c], ga_s.at[t, d], ga_r.at[t, q])
        for d in (1, 2, 3):
            push(jj_ref.at[k, r], jj_ref.at[k, r], gb_s.at[t, d], gb_r.at[t, x], at_x(d))

    def phase_i(t):
        for d in (1, 2, 3):
            q = (x + d) % 4
            arrived(jj_ref.at[k, pl.ds(tile_row(t, q, y), 8)], gb_s.at[t, d], gb_r.at[t, q])
        r = pl.ds(pl.multiple_of(t * 128 + y * 32, 32), 32)
        for d in (1, 2, 3):
            push(jj_ref.at[k, r], jj_ref.at[k, r], gc_s.at[t, d], gc_r.at[t, y], at_y(d))

    def phase_j(t):
        for d in (1, 2, 3):
            q = (y + d) % 4
            arrived(jj_ref.at[k, pl.ds(pl.multiple_of(t * 128 + q * 32, 32), 32)], gc_s.at[t, d], gc_r.at[t, q])
        r = slice(t * 128, t * 128 + 128)
        push(jj_ref.at[k, r], jj_ref.at[k, r], gd_s.at[t], gd_r.at[t], partner)

    def phase_k(t):
        for d in (1, 2, 3):
            q = (y + d) % 4
            arrived(yf.at[t, q], b_s.at[t, d], b_r.at[t, q])
        for j in range(2):
            v = yf[t, :, j].reshape(128, 512) * (-mask_ref[j, 0:1, :])
            v = v.T
            for i in range(4):
                sj_ref[j, i, :, t * 128 : (t + 1) * 128] = v[i * 128 : (i + 1) * 128]

    def phase_l(t):
        arrived(jj_ref.at[other, t * 128 : t * 128 + 128], gd_s.at[t], gd_r.at[t])

    phases = dict(
        o=phase_o, p=phase_p, v=phase_v, b=phase_b, c=phase_c, d=phase_d, e=phase_e, f=phase_f, g=phase_g,
        h=phase_h, i=phase_i, j=phase_j, k=phase_k, l=phase_l, m=phase_m,
    )
    for name, t in ORDER:
        phases[name](t)

    for copy in sent:
        copy.wait_send()

    @pl.when(k != zl)
    def _():
        for t in range(CH):
            remote(yts.at[t], yf.at[t, y, k], a_s.at[t, 0], a_r.at[t, k], partner).wait_send()


def local(sigma_anc, panel, pattern, linv):
    row_ids = jnp.arange(4, dtype=jnp.int32) * 32 + lax.axis_index("row")
    in_pattern = jnp.any(pattern[:, :, None] == row_ids[None, None, :], axis=1).astype(F32)
    mask = jnp.broadcast_to(in_pattern[:, None, :, None], (2, 8, 4, 128)).reshape(2, 8, 512)
    s = sigma_anc.reshape(4, 4, 4, 128, 128)
    dma = pltpu.SemaphoreType.DMA
    vm = lambda *shape: pltpu.VMEM(shape, F32)
    vb = lambda *shape: pltpu.VMEM(shape, BF)
    pair = lambda *shape: [dma(shape), dma(shape)]
    return pl.pallas_call(
        kernel,
        out_shape=(
            jax.ShapeDtypeStruct((2, 4, 128, 512), F32),
            jax.ShapeDtypeStruct((2, 512, 512), F32),
        ),
        in_specs=[pl.BlockSpec(memory_space=pl.ANY)] + [pl.BlockSpec(memory_space=pltpu.VMEM)] * 3,
        out_specs=[pl.BlockSpec(memory_space=pltpu.VMEM)] * 2,
        scratch_shapes=[
            vm(4, 4, 4, 128, 128), vm(4, 4, 4, 128, 128),
            vb(4, 2048, 512), vm(512, 512), vm(512, 512), vm(512, 512), vb(512, 2048), vb(2, 512, 512),
            vm(CH, 32, 512), vm(4, 512, 512), vm(CH, 2, 64, 512), vm(CH, 2, 128, 512),
            vm(CH, 4, 32, 512), vm(CH, 4, 32, 512), vm(CH, 32, 512), vm(CH, 4, 2, 32, 512),
            vm(CH, 32, 512), vm(CH, 4, 8, 512), vm(CH, 4, 8, 128), vm(CH, 8, 8, 128),
            dma((4,)), *pair(4), *pair(1), *pair(CH, 2), *pair(CH, 2), *pair(CH, 4), *pair(CH, 4),
            *pair(CH, 2), *pair(CH, 4), *pair(CH, 4), *pair(CH, 8), *pair(CH, 4), *pair(CH, 4), *pair(CH, 4), *pair(CH),
        ],
        compiler_params=pltpu.CompilerParams(
            collective_id=0, has_side_effects=True, vmem_limit_bytes=60 << 20
        ),
        name="selinv",
    )(s, panel.reshape(2, 512, 512), linv, mask)


def solution(mesh):
    return jax.shard_map(
        local,
        mesh=mesh,
        in_specs=(P("row", "col", None, None), P(None, "row", None, None), P(), P()),
        out_specs=(P(None, "row", None, None), P()),
        check_vma=False,
    )
```

```python
import jax
import jax.numpy as jnp
from jax import lax
from jax.experimental import pallas as pl
from jax.experimental.pallas import tpu as pltpu
from jax.sharding import PartitionSpec as P

MESH = pl.DeviceIdType.MESH
BF = jnp.bfloat16
F32 = jnp.float32
CH = 4
ORDER = (
    ("p", 0), ("o", 0), ("o", 1), ("p", 1), ("p", 2), ("b", 0), ("o", 2), ("b", 1),
    ("o", 3), ("p", 3), ("v", 0), ("c", 0), ("b", 2), ("d", 0), ("b", 3), ("c", 1),
    ("d", 1), ("e", 0), ("c", 2), ("d", 2), ("m", 0), ("e", 1), ("f", 0), ("c", 3),
    ("d", 3), ("m", 1), ("e", 2), ("k", 0), ("g", 0), ("m", 2), ("f", 1), ("g", 1),
    ("h", 0), ("l", 0), ("e", 3), ("f", 2), ("m", 3), ("k", 1), ("g", 2), ("h", 1),
    ("l", 1), ("f", 3), ("g", 3), ("k", 2), ("h", 2), ("l", 2), ("h", 3), ("k", 3),
    ("l", 3),
)
NN = (((1,), (0,)), ((), ()))


def split(v):
    hi = v.astype(BF)
    return hi, (v - hi.astype(F32)).astype(BF)


def dot3(a, b, dims=NN):
    dot = lambda p, q: lax.dot_general(p, q, dims, preferred_element_type=F32)
    return dot(a[0], b[0]) + (dot(a[0], b[1]) + dot(a[1], b[0]))


def kernel(
    s_ref, panel_ref, linv_ref, mask_ref, sj_ref, jj_ref,
    pbuf, lbuf, sjv, jjv, so, sp, scat, uto, uts, utp, ucat, gu, bs,
    tt, ol, nl, yl, zl_, yts, yf, gs, gx, gzl,
    in_s, out_s, s_loc, s_s, s_r, u_s, u_r, o_s, o_r, n_s, n_r, y_s, y_r, z_s, z_r,
    a_s, a_r, b_s, b_r, gx_s, gx_r, gz_s, gz_r, gb_s, gb_r, gd_s, gd_r,
):
    row = lax.axis_index("row")
    col = lax.axis_index("col")
    x, zh, k = row // 8, (row // 2) % 4, row % 2
    y, zl = col // 2, col % 2
    z = zh * 2 + zl
    other = 1 - k

    def dev(x, y, zh, zl, k):
        return ((x * 4 + zh) * 2 + k, y * 2 + zl)

    def at_x(d):
        return dev((x + d) % 4, y, zh, zl, k)

    def at_y(d):
        return dev(x, (y + d) % 4, zh, zl, k)

    def at_zh(d):
        return dev(x, y, (zh + d) % 4, zl, k)

    def at_z(d):
        t = (z + d) % 8
        return dev(x, y, t // 2, t % 2, k)

    partner = dev(x, y, zh, zl, other)
    cross = dev(x, y, zh, 1 - zl, other)
    peers = [partner, cross]
    peers += [at_z(d) for d in range(1, 8)]
    peers += [dev((x + n // 4) % 4, (y + n % 4) % 4, zh, zl, k) for n in range(1, 16)]

    sent, outs = [], []

    def remote(src, dst, send, recv, device):
        return pltpu.make_async_remote_copy(
            src_ref=src, dst_ref=dst, send_sem=send, recv_sem=recv, device_id=device, device_id_type=MESH
        )

    def push(src, dst, send, recv, device):
        copy = remote(src, dst, send, recv, device)
        copy.start()
        sent.append(copy)

    def arrived(dst, send, recv):
        remote(dst, dst, send, recv, partner).wait_recv()

    barrier = pltpu.get_barrier_semaphore()
    for peer in peers:
        pl.semaphore_signal(barrier, inc=1, device_id=peer, device_id_type=MESH)

    loads = []
    for n, j in enumerate((other, k)):
        for m, (src, dst) in enumerate(((panel_ref, pbuf), (linv_ref, lbuf))):
            copy = pltpu.make_async_copy(src.at[j], dst.at[j], in_s.at[n, m])
            copy.start()
            loads.append(copy)

    offs = (2, 1, 3, 0)
    local = []
    for p in range(4):
        copy = pltpu.make_async_copy(s_ref.at[:, :, (x + offs[p]) % 4], so.at[p], s_loc.at[p])
        copy.start()
        local.append(copy)

    def update(j):
        a = split(pbuf[j])
        b = split(lbuf[j])
        return dot3(a, b).T * mask_ref[j, 0:1, :]

    loads[0].wait()
    loads[1].wait()
    uts[...] = update(other)
    pl.semaphore_wait(barrier, len(peers))
    for p in range(4):
        local[p].wait()
        push(so.at[p], sp.at[p], s_s.at[p], s_r.at[p], partner)
        if p == 0:
            push(uts, utp, u_s.at[0], u_r.at[0], partner)
    loads[2].wait()
    loads[3].wait()
    ut = update(k)
    uto[...] = ut
    ucat[:, 0:512], ucat[:, 1024:1536] = split(ut)

    def spread(p, half, src):
        def body(i, carry):
            r = pl.multiple_of(half * 512 + i * 128, 128)
            for m in range(4):
                hi, lo = split(src[p, i, m])
                scat[p, pl.ds(r, 128), m * 128 : (m + 1) * 128] = lo
                scat[p, pl.ds(1024 + r, 128), m * 128 : (m + 1) * 128] = hi
            return carry

        lax.fori_loop(0, 4, body, 0)

    def phase_p(p):
        spread(p, 0, so)
        if p == 0:
            arrived(utp, u_s.at[0], u_r.at[0])
            ucat[:, 512:1024], ucat[:, 1536:2048] = split(utp[...])
        arrived(sp.at[p], s_s.at[p], s_r.at[p])
        spread(p, 1, sp)
        dot = lambda a, b: jnp.dot(a, b, preferred_element_type=F32)
        tt[p] = dot(ucat[...], scat[p]) + dot(ucat[:, 0:1024], scat[p, 1024:2048])

    def phase_o(t):
        r = t * 128
        push(tt.at[0, r : r + 64], ol.at[t, 0], o_s.at[t, 0], o_r.at[t, 0], at_x(1))
        push(tt.at[0, r + 64 : r + 128], ol.at[t, 1], o_s.at[t, 1], o_r.at[t, 1], at_x(3))

    def phase_v(t):
        @pl.when(k == zl)
        def _():
            gu[0], gu[1] = split(uto[...].T)

        @pl.when(k != zl)
        def _():
            gu[0], gu[1] = split(utp[...].T)

        uto[...] = lbuf[k].T
        first = jnp.where((x == 0) & (z == 0), 1.0, 0.0).astype(F32)
        rows = [uto[pl.ds(pl.multiple_of(t * 128 + y * 32, 32), 32)] for t in range(CH)]
        base = dot3(split(jnp.concatenate(rows)), split(lbuf[k])) * first
        for t in range(CH):
            bs[t] = base[t * 32 : t * 32 + 32]

    def phase_b(t):
        for s in (0, 1):
            arrived(ol.at[t, s], o_s.at[t, s], o_r.at[t, s])
            r = slice(t * 128 + s * 64, t * 128 + s * 64 + 64)
            tt[1 + s, r] = tt[1 + s, r] + ol[t, s]
            push(tt.at[1 + s, t * 128 : t * 128 + 128], nl.at[t, s], n_s.at[t, s], n_r.at[t, s], at_x(1 + 2 * s))

    def phase_c(t):
        for s in (0, 1):
            arrived(nl.at[t, s], n_s.at[t, s], n_r.at[t, s])
        r = slice(t * 128, t * 128 + 128)
        tt[3, r] = tt[3, r] + (nl[t, 0] + nl[t, 1])
        for d in (1, 2, 3):
            q = (y + d) % 4
            push(tt.at[3, pl.ds(pl.multiple_of(t * 128 + q * 32, 32), 32)], yl.at[t, y], y_s.at[t, d], y_r.at[t, y], at_y(d))
        yl[t, y] = tt[3, pl.ds(pl.multiple_of(t * 128 + y * 32, 32), 32)]

    def phase_d(t):
        for d in (1, 2, 3):
            q = (y + d) % 4
            arrived(yl.at[t, q], y_s.at[t, d], y_r.at[t, q])
        for d in (1, 2, 3):
            q = (zh + d) % 4
            push(yl.at[t, q], zl_.at[t, zh], z_s.at[t, d], z_r.at[t, zh], at_zh(d))

    def phase_e(t):
        yt = yl[t, zh]
        for d in (1, 2, 3):
            q = (zh + d) % 4
            arrived(zl_.at[t, q], z_s.at[t, d], z_r.at[t, q])
            yt = yt + zl_[t, q]
        yts[t] = yt

        @pl.when(k == zl)
        def _():
            yf[t, y, k] = yt

        @pl.when(k != zl)
        def _():
            remote(yts.at[t], yf.at[t, y, k], a_s.at[t, 0], a_r.at[t, k], partner).start()

        push(yts.at[t], yf.at[t, y, k], a_s.at[t, 1], a_r.at[t, k], dev(x, y, zh, 1 - zl, zl))
        yh, yl_ = split(yt)
        c = slice(t * 128, 512)
        g = jnp.dot(jnp.concatenate([yh, yl_]), gu[0, :, c], preferred_element_type=F32)
        g2 = jnp.dot(yh, gu[1, :, c], preferred_element_type=F32)
        gs[t, :, c] = (g[0:32] + bs[t, :, c]) + (g[32:64] + g2)
        for d in (1, 2, 3):
            r = pl.ds(pl.multiple_of((x + d) % 4 * 8, 8), 8)
            push(gs.at[t, r, c], gx.at[t, x, :, c], gx_s.at[t, d], gx_r.at[t, x], at_x(d))

    def phase_f(t):
        arrived(yf.at[t, y, other], a_s.at[t, 0], a_r.at[t, other])

        @pl.when(k != zl)
        def _():
            arrived(yf.at[t, y, k], a_s.at[t, 0], a_r.at[t, k])

        for d in (1, 2, 3):
            push(yf.at[t, y], yf.at[t, y], b_s.at[t, d], b_r.at[t, y], at_y(d))
    def phase_m(t):
        c = slice(t * 128, 512)
        g = gs[t, pl.ds(pl.multiple_of(x * 8, 8), 8), c]
        for d in (1, 2, 3):
            q = (x + d) % 4
            arrived(gx.at[t, q, :, c], gx_s.at[t, d], gx_r.at[t, q])
            g = g + gx[t, q, :, c]
        gzl[t, z, :, c] = g
        for d in range(1, 8):
            push(gzl.at[t, z, :, c], gzl.at[t, z, :, c], gz_s.at[t, d], gz_r.at[t, z], at_z(d))

    def tile_row(t, x, y):
        return pl.ds(pl.multiple_of(t * 128 + y * 32 + x * 8, 8), 8)

    def phase_g(t):
        c = slice(t * 128, 512)
        for d in range(1, 8):
            q = (z + d) % 8
            arrived(gzl.at[t, q, :, c], gz_s.at[t, d], gz_r.at[t, q])
        g = gzl[t, 0, :, c]
        for q in range(1, 8):
            g = g + gzl[t, q, :, c]
        r = tile_row(t, x, y)
        jjv[k, r, c] = g
        for n in range(1, 16):
            dx, dy = n // 4, n % 4
            push(
                jjv.at[k, r, c], jjv.at[k, r, c], gb_s.at[t, n], gb_r.at[t, x * 4 + y],
                dev((x + dx) % 4, (y + dy) % 4, zh, zl, k),
            )

    def store(t, j, side):
        r, c = slice(t * 128, t * 128 + 128), slice(t * 128, 512)
        if side:
            r, c = slice(t * 128 + 128, 512), r
        copy = pltpu.make_async_copy(jjv.at[j, r, c], jj_ref.at[j, r, c], out_s.at[t, side, j])
        copy.start()
        outs.append(copy)

    def mirror(t, j):
        r = slice(t * 128, t * 128 + 128)
        for n in range(t + 1, 4):
            c = slice(n * 128, n * 128 + 128)
            jjv[j, c, r] = jjv[j, r, c].T

    def phase_h(t):
        r, c = slice(t * 128, t * 128 + 128), slice(t * 128, 512)
        for n in range(1, 16):
            dx, dy = n // 4, n % 4
            qx, qy = (x + dx) % 4, (y + dy) % 4
            arrived(jjv.at[k, tile_row(t, qx, qy), c], gb_s.at[t, n], gb_r.at[t, qx * 4 + qy])
        push(jjv.at[k, r, c], jjv.at[k, r, c], gd_s.at[t], gd_r.at[t], partner)

    def phase_k(t):
        for d in (1, 2, 3):
            q = (y + d) % 4
            arrived(yf.at[t, q], b_s.at[t, d], b_r.at[t, q])
        for j in range(2):
            v = yf[t, :, j].reshape(128, 512) * (-mask_ref[j, 0:1, :])
            v = v.T
            for i in range(4):
                sjv[j, i, :, t * 128 : (t + 1) * 128] = v[i * 128 : (i + 1) * 128]
        c = slice(t * 128, t * 128 + 128)
        copy = pltpu.make_async_copy(sjv.at[:, :, :, c], sj_ref.at[:, :, :, c], out_s.at[t, 2, 0])
        copy.start()
        outs.append(copy)

    def phase_l(t):
        r, c = slice(t * 128, t * 128 + 128), slice(t * 128, 512)
        arrived(jjv.at[other, r, c], gd_s.at[t], gd_r.at[t])
        for j in range(2):
            store(t, j, 0)
            if t < 3:
                mirror(t, j)
                store(t, j, 1)

    phases = dict(
        o=phase_o, p=phase_p, v=phase_v, b=phase_b, c=phase_c, d=phase_d, e=phase_e, f=phase_f, g=phase_g,
        h=phase_h, k=phase_k, l=phase_l, m=phase_m,
    )
    for name, t in ORDER:
        phases[name](t)

    for copy in sent:
        copy.wait_send()
    for copy in outs:
        copy.wait()

    @pl.when(k != zl)
    def _():
        for t in range(CH):
            remote(yts.at[t], yf.at[t, y, k], a_s.at[t, 0], a_r.at[t, k], partner).wait_send()


def local(sigma_anc, panel, pattern, linv):
    row_ids = jnp.arange(4, dtype=jnp.int32) * 32 + lax.axis_index("row")
    in_pattern = jnp.any(pattern[:, :, None] == row_ids[None, None, :], axis=1).astype(F32)
    mask = jnp.broadcast_to(in_pattern[:, None, :, None], (2, 8, 4, 128)).reshape(2, 8, 512)
    s = sigma_anc.reshape(4, 4, 4, 128, 128)
    dma = pltpu.SemaphoreType.DMA
    vm = lambda *shape: pltpu.VMEM(shape, F32)
    vb = lambda *shape: pltpu.VMEM(shape, BF)
    pair = lambda *shape: [dma(shape), dma(shape)]
    return pl.pallas_call(
        kernel,
        out_shape=(
            jax.ShapeDtypeStruct((2, 4, 128, 512), F32),
            jax.ShapeDtypeStruct((2, 512, 512), F32),
        ),
        in_specs=[pl.BlockSpec(memory_space=pl.ANY)] * 3 + [pl.BlockSpec(memory_space=pltpu.VMEM)],
        out_specs=[pl.BlockSpec(memory_space=pl.ANY)] * 2,
        scratch_shapes=[
            vm(2, 512, 512), vm(2, 512, 512), vm(2, 4, 128, 512), vm(2, 512, 512),
            vm(4, 4, 4, 128, 128), vm(4, 4, 4, 128, 128),
            vb(4, 2048, 512), vm(512, 512), vm(512, 512), vm(512, 512), vb(512, 2048), vb(2, 512, 512),
            vm(CH, 32, 512), vm(4, 512, 512), vm(CH, 2, 64, 512), vm(CH, 2, 128, 512),
            vm(CH, 4, 32, 512), vm(CH, 4, 32, 512), vm(CH, 32, 512), vm(CH, 4, 2, 32, 512),
            vm(CH, 32, 512), vm(CH, 4, 8, 512), vm(CH, 8, 8, 512),
            dma((2, 2)), dma((CH, 3, 2)), dma((4,)), *pair(4), *pair(1), *pair(CH, 2), *pair(CH, 2), *pair(CH, 4), *pair(CH, 4),
            *pair(CH, 2), *pair(CH, 4), *pair(CH, 4), *pair(CH, 8), *pair(CH, 16), *pair(CH),
        ],
        compiler_params=pltpu.CompilerParams(
            collective_id=0, has_side_effects=True, vmem_limit_bytes=60 << 20
        ),
        name="selinv",
    )(s, panel.reshape(2, 512, 512), linv, mask)


def solution(mesh):
    return jax.shard_map(
        local,
        mesh=mesh,
        in_specs=(P("row", "col", None, None), P(None, "row", None, None), P(), P()),
        out_specs=(P(None, "row", None, None), P()),
        check_vma=False,
    )
```

```python
import jax
import jax.numpy as jnp
from jax import lax
from jax.experimental import pallas as pl
from jax.experimental.pallas import tpu as pltpu
from jax.sharding import PartitionSpec as P

MESH = pl.DeviceIdType.MESH
BF = jnp.bfloat16
F32 = jnp.float32
CH = 4
ORDER = (
    ("q", 0), ("o", 0), ("o", 1), ("q", 1), ("o", 2), ("p", 1), ("p", 2), ("b", 0),
    ("o", 3), ("b", 1), ("p", 3), ("v", 0), ("c", 0), ("b", 2), ("d", 0), ("b", 3),
    ("c", 1), ("d", 1), ("e", 0), ("c", 2), ("d", 2), ("m", 0), ("e", 1), ("f", 0),
    ("c", 3), ("d", 3), ("m", 1), ("e", 2), ("f", 1), ("k", 0), ("g", 0), ("m", 2),
    ("f", 2), ("e", 3), ("g", 1), ("m", 3), ("f", 3), ("h", 0), ("l", 0), ("g", 2),
    ("g", 3), ("h", 1), ("l", 1), ("k", 1), ("h", 2), ("l", 2), ("h", 3), ("l", 3),
    ("k", 2), ("k", 3),
)
NN = (((1,), (0,)), ((), ()))


def split(v):
    hi = v.astype(BF)
    return hi, (v - hi.astype(F32)).astype(BF)


def dot3(a, b, dims=NN):
    dot = lambda p, q: lax.dot_general(p, q, dims, preferred_element_type=F32)
    return dot(a[0], b[0]) + (dot(a[0], b[1]) + dot(a[1], b[0]))


def kernel(
    s_ref, panel_ref, linv_ref, pattern_ref, sj_ref, jj_ref,
    mask_ref, pbuf, lbuf, sjv, jjv, so, sp, scat, uto, uts, utp, ucat, gu, bs,
    tt, ol, nl, yl, zl_, yts, yf, gs, gx, gzl,
    in_s, out_s, s_loc, s_s, s_r, u_s, u_r, o_s, o_r, n_s, n_r, y_s, y_r, z_s, z_r,
    a_s, a_r, b_s, b_r, gx_s, gx_r, gz_s, gz_r, gb_s, gb_r, gd_s, gd_r,
):
    row = lax.axis_index("row")
    col = lax.axis_index("col")
    x, zh, k = row // 8, (row // 2) % 4, row % 2
    y, zl = col // 2, col % 2
    z = zh * 2 + zl
    other = 1 - k

    def dev(x, y, zh, zl, k):
        return ((x * 4 + zh) * 2 + k, y * 2 + zl)

    def at_x(d):
        return dev((x + d) % 4, y, zh, zl, k)

    def at_y(d):
        return dev(x, (y + d) % 4, zh, zl, k)

    def at_zh(d):
        return dev(x, y, (zh + d) % 4, zl, k)

    def at_z(d):
        t = (z + d) % 8
        return dev(x, y, t // 2, t % 2, k)

    partner = dev(x, y, zh, zl, other)
    cross = dev(x, y, zh, 1 - zl, other)
    peers = [partner, cross]
    peers += [at_z(d) for d in range(1, 8)]
    peers += [dev((x + n // 4) % 4, (y + n % 4) % 4, zh, zl, k) for n in range(1, 16)]

    sent, outs = [], []

    def remote(src, dst, send, recv, device):
        return pltpu.make_async_remote_copy(
            src_ref=src, dst_ref=dst, send_sem=send, recv_sem=recv, device_id=device, device_id_type=MESH
        )

    def push(src, dst, send, recv, device):
        copy = remote(src, dst, send, recv, device)
        copy.start()
        sent.append(copy)

    def arrived(dst, send, recv):
        remote(dst, dst, send, recv, partner).wait_recv()

    barrier = pltpu.get_barrier_semaphore()
    for peer in peers:
        pl.semaphore_signal(barrier, inc=1, device_id=peer, device_id_type=MESH)

    loads = []
    for n, j in enumerate((other, k)):
        for m, (src, dst) in enumerate(((panel_ref, pbuf), (linv_ref, lbuf))):
            copy = pltpu.make_async_copy(src.at[j], dst.at[j], in_s.at[n, m])
            copy.start()
            loads.append(copy)

    offs = (2, 1, 3, 0)
    local = []
    for p in range(4):
        copy = pltpu.make_async_copy(s_ref.at[:, :, (x + offs[p]) % 4], so.at[p], s_loc.at[p])
        copy.start()
        local.append(copy)

    pattern = pattern_ref[...]
    for i in range(4):
        hit = jnp.where(pattern == i * 32 + row, 1.0, 0.0).astype(F32)
        for j in range(2):
            value = jnp.max(hit[j : j + 1], axis=1, keepdims=True)
            mask_ref[j, :, i * 128 : (i + 1) * 128] = jnp.broadcast_to(value, (8, 128))

    def update(j, a, h):
        b = split(lbuf[j, h * 256 : 512, h * 256 : h * 256 + 256])
        a = tuple(v[:, h * 256 :] for v in a)
        return dot3(a, b).T * mask_ref[j, 0:1, :]

    def update_other(h):
        r = slice(h * 256, h * 256 + 256)
        uts[r] = update(other, panel_other, h)

    def push_other(h):
        r = slice(h * 256, h * 256 + 256)
        push(uts.at[r], utp.at[r], u_s.at[h], u_r.at[h], partner)

    def update_own(h):
        r = slice(h * 256, h * 256 + 256)
        ut = update(k, panel_own, h)
        uto[r] = ut
        ucat[r, 0:512], ucat[r, 1024:1536] = split(ut)

    def receive(h):
        r = slice(h * 256, h * 256 + 256)
        arrived(utp.at[r], u_s.at[h], u_r.at[h])
        ucat[r, 512:1024], ucat[r, 1536:2048] = split(utp[r])

    loads[0].wait()
    loads[1].wait()
    panel_other = split(pbuf[other])
    update_other(0)
    pl.semaphore_wait(barrier, len(peers))
    for p in range(4):
        local[p].wait()
        push(so.at[p], sp.at[p], s_s.at[p], s_r.at[p], partner)
        if p == 0:
            push_other(0)
    loads[2].wait()
    loads[3].wait()
    panel_own = split(pbuf[k])
    update_own(0)

    def spread(p, half, src):
        def body(i, carry):
            r = pl.multiple_of(half * 512 + i * 128, 128)
            for m in range(4):
                hi, lo = split(src[p, i, m])
                scat[p, pl.ds(r, 128), m * 128 : (m + 1) * 128] = lo
                scat[p, pl.ds(1024 + r, 128), m * 128 : (m + 1) * 128] = hi
            return carry

        lax.fori_loop(0, 4, body, 0)

    def multiply(p, r):
        dot = lambda a, b: jnp.dot(a, b, preferred_element_type=F32)
        tt[p, r] = dot(ucat[r], scat[p]) + dot(ucat[r, 0:1024], scat[p, 1024:2048])

    def phase_q(h):
        if h == 0:
            spread(0, 0, so)
        else:
            update_other(1)
            push_other(1)
            update_own(1)
        receive(h)
        if h == 0:
            arrived(sp.at[0], s_s.at[0], s_r.at[0])
            spread(0, 1, sp)
        multiply(0, slice(h * 256, h * 256 + 256))

    def phase_p(p):
        spread(p, 0, so)
        arrived(sp.at[p], s_s.at[p], s_r.at[p])
        spread(p, 1, sp)
        multiply(p, slice(0, 512))

    def phase_o(t):
        r = t * 128
        push(tt.at[0, r : r + 64], ol.at[t, 0], o_s.at[t, 0], o_r.at[t, 0], at_x(1))
        push(tt.at[0, r + 64 : r + 128], ol.at[t, 1], o_s.at[t, 1], o_r.at[t, 1], at_x(3))

    def phase_v(t):
        @pl.when(k == zl)
        def _():
            gu[0], gu[1] = split(uto[...].T)

        @pl.when(k != zl)
        def _():
            gu[0], gu[1] = split(utp[...].T)

        uto[...] = lbuf[k].T
        first = jnp.where((x == 0) & (z == 0), 1.0, 0.0).astype(F32)
        rows = [uto[pl.ds(pl.multiple_of(t * 128 + y * 32, 32), 32)] for t in range(CH)]
        base = dot3(split(jnp.concatenate(rows)), split(lbuf[k])) * first
        for t in range(CH):
            bs[t] = base[t * 32 : t * 32 + 32]

    def phase_b(t):
        for s in (0, 1):
            arrived(ol.at[t, s], o_s.at[t, s], o_r.at[t, s])
            r = slice(t * 128 + s * 64, t * 128 + s * 64 + 64)
            tt[1 + s, r] = tt[1 + s, r] + ol[t, s]
            push(tt.at[1 + s, t * 128 : t * 128 + 128], nl.at[t, s], n_s.at[t, s], n_r.at[t, s], at_x(1 + 2 * s))

    def phase_c(t):
        for s in (0, 1):
            arrived(nl.at[t, s], n_s.at[t, s], n_r.at[t, s])
        r = slice(t * 128, t * 128 + 128)
        tt[3, r] = tt[3, r] + (nl[t, 0] + nl[t, 1])
        for d in (1, 2, 3):
            q = (y + d) % 4
            push(tt.at[3, pl.ds(pl.multiple_of(t * 128 + q * 32, 32), 32)], yl.at[t, y], y_s.at[t, d], y_r.at[t, y], at_y(d))
        yl[t, y] = tt[3, pl.ds(pl.multiple_of(t * 128 + y * 32, 32), 32)]

    def phase_d(t):
        for d in (1, 2, 3):
            q = (y + d) % 4
            arrived(yl.at[t, q], y_s.at[t, d], y_r.at[t, q])
        for d in (1, 2, 3):
            q = (zh + d) % 4
            push(yl.at[t, q], zl_.at[t, zh], z_s.at[t, d], z_r.at[t, zh], at_zh(d))

    def phase_e(t):
        yt = yl[t, zh]
        for d in (1, 2, 3):
            q = (zh + d) % 4
            arrived(zl_.at[t, q], z_s.at[t, d], z_r.at[t, q])
            yt = yt + zl_[t, q]
        yts[t] = yt

        @pl.when(k == zl)
        def _():
            yf[t, y, k] = yt

        @pl.when(k != zl)
        def _():
            remote(yts.at[t], yf.at[t, y, k], a_s.at[t, 0], a_r.at[t, k], partner).start()

        push(yts.at[t], yf.at[t, y, k], a_s.at[t, 1], a_r.at[t, k], dev(x, y, zh, 1 - zl, zl))
        yh, yl_ = split(yt)
        c = slice(t * 128, 512)
        g = jnp.dot(jnp.concatenate([yh, yl_]), gu[0, :, c], preferred_element_type=F32)
        g2 = jnp.dot(yh, gu[1, :, c], preferred_element_type=F32)
        gs[t, :, c] = (g[0:32] + bs[t, :, c]) + (g[32:64] + g2)
        for d in (1, 2, 3):
            r = pl.ds(pl.multiple_of((x + d) % 4 * 8, 8), 8)
            push(gs.at[t, r, c], gx.at[t, x, :, c], gx_s.at[t, d], gx_r.at[t, x], at_x(d))

    def phase_f(t):
        arrived(yf.at[t, y, other], a_s.at[t, 0], a_r.at[t, other])

        @pl.when(k != zl)
        def _():
            arrived(yf.at[t, y, k], a_s.at[t, 0], a_r.at[t, k])

        for d in (1, 2, 3):
            push(yf.at[t, y], yf.at[t, y], b_s.at[t, d], b_r.at[t, y], at_y(d))
    def phase_m(t):
        c = slice(t * 128, 512)
        g = gs[t, pl.ds(pl.multiple_of(x * 8, 8), 8), c]
        for d in (1, 2, 3):
            q = (x + d) % 4
            arrived(gx.at[t, q, :, c], gx_s.at[t, d], gx_r.at[t, q])
            g = g + gx[t, q, :, c]
        gzl[t, z, :, c] = g
        for d in range(1, 8):
            push(gzl.at[t, z, :, c], gzl.at[t, z, :, c], gz_s.at[t, d], gz_r.at[t, z], at_z(d))

    def tile_row(t, x, y):
        return pl.ds(pl.multiple_of(t * 128 + y * 32 + x * 8, 8), 8)

    def phase_g(t):
        c = slice(t * 128, 512)
        for d in range(1, 8):
            q = (z + d) % 8
            arrived(gzl.at[t, q, :, c], gz_s.at[t, d], gz_r.at[t, q])
        g = gzl[t, 0, :, c]
        for q in range(1, 8):
            g = g + gzl[t, q, :, c]
        r = tile_row(t, x, y)
        jjv[k, r, c] = g
        for n in range(1, 16):
            dx, dy = n // 4, n % 4
            push(
                jjv.at[k, r, c], jjv.at[k, r, c], gb_s.at[t, n], gb_r.at[t, x * 4 + y],
                dev((x + dx) % 4, (y + dy) % 4, zh, zl, k),
            )

    def store(t, j, side):
        r, c = slice(t * 128, t * 128 + 128), slice(t * 128, 512)
        if side:
            r, c = slice(t * 128 + 128, 512), r
        copy = pltpu.make_async_copy(jjv.at[j, r, c], jj_ref.at[j, r, c], out_s.at[t, side, j])
        copy.start()
        outs.append(copy)

    def mirror(t, j):
        r = slice(t * 128, t * 128 + 128)
        for n in range(t + 1, 4):
            c = slice(n * 128, n * 128 + 128)
            jjv[j, c, r] = jjv[j, r, c].T

    def phase_h(t):
        r, c = slice(t * 128, t * 128 + 128), slice(t * 128, 512)
        for n in range(1, 16):
            dx, dy = n // 4, n % 4
            qx, qy = (x + dx) % 4, (y + dy) % 4
            arrived(jjv.at[k, tile_row(t, qx, qy), c], gb_s.at[t, n], gb_r.at[t, qx * 4 + qy])
        push(jjv.at[k, r, c], jjv.at[k, r, c], gd_s.at[t], gd_r.at[t], partner)

    def phase_k(t):
        for d in (1, 2, 3):
            q = (y + d) % 4
            arrived(yf.at[t, q], b_s.at[t, d], b_r.at[t, q])
        for j in range(2):
            v = yf[t, :, j].reshape(128, 512) * (-mask_ref[j, 0:1, :])
            v = v.T
            for i in range(4):
                sjv[j, i, :, t * 128 : (t + 1) * 128] = v[i * 128 : (i + 1) * 128]
        c = slice(t * 128, t * 128 + 128)
        copy = pltpu.make_async_copy(sjv.at[:, :, :, c], sj_ref.at[:, :, :, c], out_s.at[t, 2, 0])
        copy.start()
        outs.append(copy)

    def phase_l(t):
        r, c = slice(t * 128, t * 128 + 128), slice(t * 128, 512)
        arrived(jjv.at[other, r, c], gd_s.at[t], gd_r.at[t])
        for j in range(2):
            store(t, j, 0)
            if t < 3:
                mirror(t, j)
                store(t, j, 1)

    phases = dict(
        o=phase_o, p=phase_p, q=phase_q, v=phase_v, b=phase_b, c=phase_c, d=phase_d, e=phase_e, f=phase_f, g=phase_g,
        h=phase_h, k=phase_k, l=phase_l, m=phase_m,
    )
    for name, t in ORDER:
        phases[name](t)

    for copy in sent:
        copy.wait_send()
    for copy in outs:
        copy.wait()

    @pl.when(k != zl)
    def _():
        for t in range(CH):
            remote(yts.at[t], yf.at[t, y, k], a_s.at[t, 0], a_r.at[t, k], partner).wait_send()


def finish(sj_in, jj_in, sj_ref, jj_ref, sems):
    copies = []
    for j in range(2):
        for i in range(4):
            copies.append(pltpu.make_async_copy(sj_in.at[j, i], sj_ref.at[j, i], sems.at[j, i]))
            r = slice(i * 128, i * 128 + 128)
            copies.append(pltpu.make_async_copy(jj_in.at[j, r], jj_ref.at[j, r], sems.at[j, 4 + i]))
    for copy in copies:
        copy.start()
    for copy in copies:
        copy.wait()


def local(sigma_anc, panel, pattern, linv):
    s = sigma_anc.reshape(4, 4, 4, 128, 128)
    dma = pltpu.SemaphoreType.DMA
    vm = lambda *shape: pltpu.VMEM(shape, F32)
    vb = lambda *shape: pltpu.VMEM(shape, BF)
    pair = lambda *shape: [dma(shape), dma(shape)]
    results = pl.pallas_call(
        kernel,
        out_shape=(
            jax.ShapeDtypeStruct((2, 4, 128, 512), F32),
            jax.ShapeDtypeStruct((2, 512, 512), F32),
        ),
        in_specs=[pl.BlockSpec(memory_space=pl.ANY)] * 3 + [pl.BlockSpec(memory_space=pltpu.VMEM)],
        out_specs=[pl.BlockSpec(memory_space=pl.ANY)] * 2,
        scratch_shapes=[
            vm(2, 8, 512), vm(2, 512, 512), vm(2, 512, 512), vm(2, 4, 128, 512), vm(2, 512, 512),
            vm(4, 4, 4, 128, 128), vm(4, 4, 4, 128, 128),
            vb(4, 2048, 512), vm(512, 512), vm(512, 512), vm(512, 512), vb(512, 2048), vb(2, 512, 512),
            vm(CH, 32, 512), vm(4, 512, 512), vm(CH, 2, 64, 512), vm(CH, 2, 128, 512),
            vm(CH, 4, 32, 512), vm(CH, 4, 32, 512), vm(CH, 32, 512), vm(CH, 4, 2, 32, 512),
            vm(CH, 32, 512), vm(CH, 4, 8, 512), vm(CH, 8, 8, 512),
            dma((2, 2)), dma((CH, 3, 2)), dma((4,)), *pair(4), *pair(2), *pair(CH, 2), *pair(CH, 2), *pair(CH, 4), *pair(CH, 4),
            *pair(CH, 2), *pair(CH, 4), *pair(CH, 4), *pair(CH, 8), *pair(CH, 16), *pair(CH),
        ],
        compiler_params=pltpu.CompilerParams(
            collective_id=0, has_side_effects=True, vmem_limit_bytes=60 << 20
        ),
        name="selinv",
    )(s, panel.reshape(2, 512, 512), linv, pattern)
    return pl.pallas_call(
        finish,
        out_shape=tuple(jax.ShapeDtypeStruct(v.shape, F32) for v in results),
        in_specs=[pl.BlockSpec(memory_space=pl.ANY)] * 2,
        out_specs=[pl.BlockSpec(memory_space=pl.ANY)] * 2,
        scratch_shapes=[dma((2, 8))],
        name="finish",
    )(*results)


def solution(mesh):
    return jax.shard_map(
        local,
        mesh=mesh,
        in_specs=(P("row", "col", None, None), P(None, "row", None, None), P(), P()),
        out_specs=(P(None, "row", None, None), P()),
        check_vma=False,
    )
```

```python
import jax
import jax.numpy as jnp
from jax import lax
from jax.experimental import pallas as pl
from jax.experimental.pallas import tpu as pltpu
from jax.sharding import PartitionSpec as P

MESH = pl.DeviceIdType.MESH
BF = jnp.bfloat16
F32 = jnp.float32
CH = 4
ORDER = (
    ("p", 0), ("o", 0), ("o", 1), ("p", 1), ("p", 2), ("b", 0), ("o", 2), ("b", 1),
    ("o", 3), ("p", 3), ("v", 0), ("b", 2), ("c", 0), ("b", 3), ("d", 0), ("c", 1),
    ("d", 1), ("c", 2), ("e", 0), ("d", 2), ("c", 3), ("f", 0), ("e", 1), ("d", 3),
    ("f", 1), ("e", 2), ("m", 0), ("m", 1), ("f", 2), ("e", 3), ("m", 2), ("g", 0),
    ("f", 3), ("m", 3), ("g", 1), ("g", 2), ("i", 0), ("k", 0), ("g", 3), ("i", 1),
    ("i", 2), ("k", 1), ("h", 0), ("i", 3), ("h", 1), ("l", 0), ("h", 2), ("k", 2),
    ("l", 1), ("h", 3), ("l", 2), ("k", 3), ("l", 3),
)
NN = (((1,), (0,)), ((), ()))


def split(v):
    hi = v.astype(BF)
    return hi, (v - hi.astype(F32)).astype(BF)


def dot3(a, b, dims=NN):
    dot = lambda p, q: lax.dot_general(p, q, dims, preferred_element_type=F32)
    return dot(a[0], b[0]) + (dot(a[0], b[1]) + dot(a[1], b[0]))


def kernel(
    s_ref, panel_ref, linv_ref, pattern_ref, sj_ref, jj_ref,
    mask_ref, pbuf, lbuf, sjv, jjv, so, sp, scat, uto, uts, utp, ucat, gu, bs,
    tt, ol, nl, yl, zl_, yts, yf, gs, gx, gzl,
    in_s, out_s, s_loc, s_s, s_r, u_s, u_r, o_s, o_r, n_s, n_r, y_s, y_r, z_s, z_r,
    a_s, a_r, b_s, b_r, gx_s, gx_r, gz_s, gz_r, gb_s, gb_r, gd_s, gd_r,
):
    row = lax.axis_index("row")
    col = lax.axis_index("col")
    x, zh, k = row // 8, (row // 2) % 4, row % 2
    y, zl = col // 2, col % 2
    z = zh * 2 + zl
    other = 1 - k

    def dev(x, y, zh, zl, k):
        return ((x * 4 + zh) * 2 + k, y * 2 + zl)

    def at_x(d):
        return dev((x + d) % 4, y, zh, zl, k)

    def at_y(d):
        return dev(x, (y + d) % 4, zh, zl, k)

    def at_zh(d):
        return dev(x, y, (zh + d) % 4, zl, k)

    def at_z(d):
        t = (z + d) % 8
        return dev(x, y, t // 2, t % 2, k)

    partner = dev(x, y, zh, zl, other)
    cross = dev(x, y, zh, 1 - zl, other)
    peers = [partner, cross]
    peers += [at_z(d) for d in range(1, 8)]
    peers += [at_x(d) for d in (1, 2, 3)] + [at_y(d) for d in (1, 2, 3)]

    sent, outs = [], []

    def remote(src, dst, send, recv, device):
        return pltpu.make_async_remote_copy(
            src_ref=src, dst_ref=dst, send_sem=send, recv_sem=recv, device_id=device, device_id_type=MESH
        )

    def push(src, dst, send, recv, device):
        copy = remote(src, dst, send, recv, device)
        copy.start()
        sent.append(copy)

    def arrived(dst, send, recv):
        remote(dst, dst, send, recv, partner).wait_recv()

    barrier = pltpu.get_barrier_semaphore()
    for peer in peers:
        pl.semaphore_signal(barrier, inc=1, device_id=peer, device_id_type=MESH)

    loads = []
    for n, j in enumerate((other, k)):
        for m, (src, dst) in enumerate(((panel_ref, pbuf), (linv_ref, lbuf))):
            copy = pltpu.make_async_copy(src.at[j], dst.at[j], in_s.at[n, m])
            copy.start()
            loads.append(copy)

    offs = (2, 1, 3, 0)
    local = []
    for p in range(4):
        copy = pltpu.make_async_copy(s_ref.at[:, :, (x + offs[p]) % 4], so.at[p], s_loc.at[p])
        copy.start()
        local.append(copy)

    pattern = pattern_ref[...]
    for i in range(4):
        hit = jnp.where(pattern == i * 32 + row, 1.0, 0.0).astype(F32)
        for j in range(2):
            value = jnp.max(hit[j : j + 1], axis=1, keepdims=True)
            mask_ref[j, :, i * 128 : (i + 1) * 128] = jnp.broadcast_to(value, (8, 128))

    def update(j):
        a = split(pbuf[j])
        b = split(lbuf[j])
        return dot3(a, b).T * mask_ref[j, 0:1, :]

    loads[0].wait()
    loads[1].wait()
    uts[...] = update(other)
    pl.semaphore_wait(barrier, len(peers))
    for p in range(4):
        local[p].wait()
        push(so.at[p], sp.at[p], s_s.at[p], s_r.at[p], partner)
        if p == 0:
            push(uts, utp, u_s.at[0], u_r.at[0], partner)
    loads[2].wait()
    loads[3].wait()
    ut = update(k)
    uto[...] = ut
    ucat[:, 0:512], ucat[:, 1024:1536] = split(ut)

    def spread(p, half, src):
        def body(i, carry):
            r = pl.multiple_of(half * 512 + i * 128, 128)
            for m in range(4):
                hi, lo = split(src[p, i, m])
                scat[p, pl.ds(r, 128), m * 128 : (m + 1) * 128] = lo
                scat[p, pl.ds(1024 + r, 128), m * 128 : (m + 1) * 128] = hi
            return carry

        lax.fori_loop(0, 4, body, 0)

    def phase_p(p):
        spread(p, 0, so)
        if p == 0:
            arrived(utp, u_s.at[0], u_r.at[0])
            ucat[:, 512:1024], ucat[:, 1536:2048] = split(utp[...])
        arrived(sp.at[p], s_s.at[p], s_r.at[p])
        spread(p, 1, sp)
        dot = lambda a, b: jnp.dot(a, b, preferred_element_type=F32)
        tt[p] = dot(ucat[...], scat[p]) + dot(ucat[:, 0:1024], scat[p, 1024:2048])

    def phase_o(t):
        r = t * 128
        push(tt.at[0, r : r + 64], ol.at[t, 0], o_s.at[t, 0], o_r.at[t, 0], at_x(1))
        push(tt.at[0, r + 64 : r + 128], ol.at[t, 1], o_s.at[t, 1], o_r.at[t, 1], at_x(3))

    def phase_v(t):
        @pl.when(k == zl)
        def _():
            gu[0], gu[1] = split(uto[...].T)

        @pl.when(k != zl)
        def _():
            gu[0], gu[1] = split(utp[...].T)

        uto[...] = lbuf[k].T
        first = jnp.where((x == 0) & (z == 0), 1.0, 0.0).astype(F32)
        rows = [uto[pl.ds(pl.multiple_of(t * 128 + y * 32, 32), 32)] for t in range(CH)]
        base = dot3(split(jnp.concatenate(rows)), split(lbuf[k])) * first
        for t in range(CH):
            bs[t] = base[t * 32 : t * 32 + 32]

    def phase_b(t):
        for s in (0, 1):
            arrived(ol.at[t, s], o_s.at[t, s], o_r.at[t, s])
            r = slice(t * 128 + s * 64, t * 128 + s * 64 + 64)
            tt[1 + s, r] = tt[1 + s, r] + ol[t, s]
            push(tt.at[1 + s, t * 128 : t * 128 + 128], nl.at[t, s], n_s.at[t, s], n_r.at[t, s], at_x(1 + 2 * s))

    def phase_c(t):
        for s in (0, 1):
            arrived(nl.at[t, s], n_s.at[t, s], n_r.at[t, s])
        r = slice(t * 128, t * 128 + 128)
        tt[3, r] = tt[3, r] + (nl[t, 0] + nl[t, 1])
        for d in (1, 2, 3):
            q = (y + d) % 4
            push(tt.at[3, pl.ds(pl.multiple_of(t * 128 + q * 32, 32), 32)], yl.at[t, y], y_s.at[t, d], y_r.at[t, y], at_y(d))
        yl[t, y] = tt[3, pl.ds(pl.multiple_of(t * 128 + y * 32, 32), 32)]

    def phase_d(t):
        for d in (1, 2, 3):
            q = (y + d) % 4
            arrived(yl.at[t, q], y_s.at[t, d], y_r.at[t, q])
        for d in (1, 2, 3):
            q = (zh + d) % 4
            push(yl.at[t, q], zl_.at[t, zh], z_s.at[t, d], z_r.at[t, zh], at_zh(d))

    def phase_e(t):
        yt = yl[t, zh]
        for d in (1, 2, 3):
            q = (zh + d) % 4
            arrived(zl_.at[t, q], z_s.at[t, d], z_r.at[t, q])
            yt = yt + zl_[t, q]
        yts[t] = yt

        @pl.when(k == zl)
        def _():
            yf[t, y, k] = yt

        @pl.when(k != zl)
        def _():
            remote(yts.at[t], yf.at[t, y, k], a_s.at[t, 0], a_r.at[t, k], partner).start()

        push(yts.at[t], yf.at[t, y, k], a_s.at[t, 1], a_r.at[t, k], dev(x, y, zh, 1 - zl, zl))
        yh, yl_ = split(yt)
        c = slice(t * 128, 512)
        g = jnp.dot(jnp.concatenate([yh, yl_]), gu[0, :, c], preferred_element_type=F32)
        g2 = jnp.dot(yh, gu[1, :, c], preferred_element_type=F32)
        gs[t, :, c] = (g[0:32] + bs[t, :, c]) + (g[32:64] + g2)
        for d in (1, 2, 3):
            r = pl.ds(pl.multiple_of((x + d) % 4 * 8, 8), 8)
            push(gs.at[t, r, c], gx.at[t, x, :, c], gx_s.at[t, d], gx_r.at[t, x], at_x(d))

    def phase_f(t):
        arrived(yf.at[t, y, other], a_s.at[t, 0], a_r.at[t, other])

        @pl.when(k != zl)
        def _():
            arrived(yf.at[t, y, k], a_s.at[t, 0], a_r.at[t, k])

        for d in (1, 2, 3):
            push(yf.at[t, y], yf.at[t, y], b_s.at[t, d], b_r.at[t, y], at_y(d))
    def phase_m(t):
        c = slice(t * 128, 512)
        g = gs[t, pl.ds(pl.multiple_of(x * 8, 8), 8), c]
        for d in (1, 2, 3):
            q = (x + d) % 4
            arrived(gx.at[t, q, :, c], gx_s.at[t, d], gx_r.at[t, q])
            g = g + gx[t, q, :, c]
        gzl[t, z, :, c] = g
        for d in range(1, 8):
            push(gzl.at[t, z, :, c], gzl.at[t, z, :, c], gz_s.at[t, d], gz_r.at[t, z], at_z(d))

    def tile_row(t, x, y):
        return pl.ds(pl.multiple_of(t * 128 + y * 32 + x * 8, 8), 8)

    def phase_g(t):
        c = slice(t * 128, 512)
        for d in range(1, 8):
            q = (z + d) % 8
            arrived(gzl.at[t, q, :, c], gz_s.at[t, d], gz_r.at[t, q])
        g = gzl[t, 0, :, c]
        for q in range(1, 8):
            g = g + gzl[t, q, :, c]
        r = tile_row(t, x, y)
        jjv[k, r, c] = g
        for d in (1, 2, 3):
            push(jjv.at[k, r, c], jjv.at[k, r, c], gb_s.at[t, d], gb_r.at[t, x * 4 + y], at_y(d))

    def phase_i(t):
        c = slice(t * 128, 512)
        for dy in range(4):
            q = (y + dy) % 4
            r = tile_row(t, x, q)
            if dy:
                arrived(jjv.at[k, r, c], gb_s.at[t, dy], gb_r.at[t, x * 4 + q])
            for dx in (1, 2, 3):
                push(jjv.at[k, r, c], jjv.at[k, r, c], gb_s.at[t, dx * 4 + dy], gb_r.at[t, x * 4 + q], at_x(dx))

    def store(t, j, side):
        r, c = slice(t * 128, t * 128 + 128), slice(t * 128, 512)
        if side:
            r, c = slice(t * 128 + 128, 512), r
        copy = pltpu.make_async_copy(jjv.at[j, r, c], jj_ref.at[j, r, c], out_s.at[t, side, j])
        copy.start()
        outs.append(copy)

    def mirror(t, j):
        r = slice(t * 128, t * 128 + 128)
        for n in range(t + 1, 4):
            c = slice(n * 128, n * 128 + 128)
            jjv[j, c, r] = jjv[j, r, c].T

    def phase_h(t):
        r, c = slice(t * 128, t * 128 + 128), slice(t * 128, 512)
        for n in range(4, 16):
            dx, dy = n // 4, n % 4
            qx, qy = (x + dx) % 4, (y + dy) % 4
            arrived(jjv.at[k, tile_row(t, qx, qy), c], gb_s.at[t, n], gb_r.at[t, qx * 4 + qy])
        push(jjv.at[k, r, c], jjv.at[k, r, c], gd_s.at[t], gd_r.at[t], partner)

    def phase_k(t):
        for d in (1, 2, 3):
            q = (y + d) % 4
            arrived(yf.at[t, q], b_s.at[t, d], b_r.at[t, q])
        for j in range(2):
            v = yf[t, :, j].reshape(128, 512) * (-mask_ref[j, 0:1, :])
            v = v.T
            for i in range(4):
                sjv[j, i, :, t * 128 : (t + 1) * 128] = v[i * 128 : (i + 1) * 128]
        c = slice(t * 128, t * 128 + 128)
        copy = pltpu.make_async_copy(sjv.at[:, :, :, c], sj_ref.at[:, :, :, c], out_s.at[t, 2, 0])
        copy.start()
        outs.append(copy)

    def phase_l(t):
        r, c = slice(t * 128, t * 128 + 128), slice(t * 128, 512)
        arrived(jjv.at[other, r, c], gd_s.at[t], gd_r.at[t])
        for j in range(2):
            store(t, j, 0)
            if t < 3:
                mirror(t, j)
                store(t, j, 1)

    phases = dict(
        o=phase_o, p=phase_p, i=phase_i, v=phase_v, b=phase_b, c=phase_c, d=phase_d, e=phase_e, f=phase_f, g=phase_g,
        h=phase_h, k=phase_k, l=phase_l, m=phase_m,
    )
    for name, t in ORDER:
        phases[name](t)

    for copy in sent:
        copy.wait_send()
    for copy in outs:
        copy.wait()

    @pl.when(k != zl)
    def _():
        for t in range(CH):
            remote(yts.at[t], yf.at[t, y, k], a_s.at[t, 0], a_r.at[t, k], partner).wait_send()


def finish(sj_in, jj_in, sj_ref, jj_ref, sj_buf, jj_buf, in_s, out_s):
    parts = []
    for j in range(2):
        for i in range(4):
            parts.append((sj_in.at[j, i], sj_buf.at[j, i], sj_ref.at[j, i], (j, i)))
            r = slice(i * 128, i * 128 + 128)
            parts.append((jj_in.at[j, r], jj_buf.at[j, r], jj_ref.at[j, r], (j, 4 + i)))
    loads = [pltpu.make_async_copy(a, b, in_s.at[n]) for a, b, c, n in parts]
    stores = [pltpu.make_async_copy(b, c, out_s.at[n]) for a, b, c, n in parts]
    for copy in loads:
        copy.start()
    for load, store in zip(loads, stores):
        load.wait()
        store.start()
    for copy in stores:
        copy.wait()


def local(sigma_anc, panel, pattern, linv):
    s = sigma_anc.reshape(4, 4, 4, 128, 128)
    dma = pltpu.SemaphoreType.DMA
    vm = lambda *shape: pltpu.VMEM(shape, F32)
    vb = lambda *shape: pltpu.VMEM(shape, BF)
    pair = lambda *shape: [dma(shape), dma(shape)]
    results = pl.pallas_call(
        kernel,
        out_shape=(
            jax.ShapeDtypeStruct((2, 4, 128, 512), F32),
            jax.ShapeDtypeStruct((2, 512, 512), F32),
        ),
        in_specs=[pl.BlockSpec(memory_space=pl.ANY)] * 3 + [pl.BlockSpec(memory_space=pltpu.VMEM)],
        out_specs=[pl.BlockSpec(memory_space=pl.ANY)] * 2,
        scratch_shapes=[
            vm(2, 8, 512), vm(2, 512, 512), vm(2, 512, 512), vm(2, 4, 128, 512), vm(2, 512, 512),
            vm(4, 4, 4, 128, 128), vm(4, 4, 4, 128, 128),
            vb(4, 2048, 512), vm(512, 512), vm(512, 512), vm(512, 512), vb(512, 2048), vb(2, 512, 512),
            vm(CH, 32, 512), vm(4, 512, 512), vm(CH, 2, 64, 512), vm(CH, 2, 128, 512),
            vm(CH, 4, 32, 512), vm(CH, 4, 32, 512), vm(CH, 32, 512), vm(CH, 4, 2, 32, 512),
            vm(CH, 32, 512), vm(CH, 4, 8, 512), vm(CH, 8, 8, 512),
            dma((2, 2)), dma((CH, 3, 2)), dma((4,)), *pair(4), *pair(1), *pair(CH, 2), *pair(CH, 2), *pair(CH, 4), *pair(CH, 4),
            *pair(CH, 2), *pair(CH, 4), *pair(CH, 4), *pair(CH, 8), *pair(CH, 16), *pair(CH),
        ],
        compiler_params=pltpu.CompilerParams(
            collective_id=0, has_side_effects=True, vmem_limit_bytes=60 << 20
        ),
        name="selinv",
    )(s, panel.reshape(2, 512, 512), linv, pattern)
    return pl.pallas_call(
        finish,
        out_shape=tuple(jax.ShapeDtypeStruct(v.shape, F32) for v in results),
        in_specs=[pl.BlockSpec(memory_space=pl.ANY)] * 2,
        out_specs=[pl.BlockSpec(memory_space=pl.ANY)] * 2,
        scratch_shapes=[vm(2, 4, 128, 512), vm(2, 512, 512), dma((2, 8)), dma((2, 8))],
        name="finish",
    )(*results)


def solution(mesh):
    return jax.shard_map(
        local,
        mesh=mesh,
        in_specs=(P("row", "col", None, None), P(None, "row", None, None), P(), P()),
        out_specs=(P(None, "row", None, None), P()),
        check_vma=False,
    )
```

```python
import jax
import jax.numpy as jnp
from jax import lax
from jax.experimental import pallas as pl
from jax.experimental.pallas import tpu as pltpu
from jax.sharding import PartitionSpec as P

MESH = pl.DeviceIdType.MESH
BF = jnp.bfloat16
F32 = jnp.float32
CH = 4
ORDER = (
    ("p", 0), ("o", 0), ("o", 1), ("p", 1), ("p", 2), ("b", 0), ("o", 2), ("b", 1),
    ("o", 3), ("p", 3), ("v", 0), ("b", 2), ("c", 0), ("b", 3), ("d", 0), ("c", 1),
    ("d", 1), ("c", 2), ("e", 0), ("d", 2), ("c", 3), ("f", 0), ("e", 1), ("d", 3),
    ("f", 1), ("e", 2), ("m", 0), ("f", 2), ("e", 3), ("g", 0), ("m", 1), ("f", 3),
    ("i", 0), ("g", 1), ("k", 0), ("k", 1), ("h", 0), ("i", 1), ("k", 2), ("l", 0),
    ("h", 1), ("k", 3), ("l", 1),
)
NN = (((1,), (0,)), ((), ()))


def split(v):
    hi = v.astype(BF)
    return hi, (v - hi.astype(F32)).astype(BF)


def dot3(a, b, dims=NN):
    dot = lambda p, q: lax.dot_general(p, q, dims, preferred_element_type=F32)
    return dot(a[0], b[0]) + (dot(a[0], b[1]) + dot(a[1], b[0]))


def kernel(
    s_ref, panel_ref, linv_ref, pattern_ref, sj_ref, jj_ref,
    mask_ref, pbuf, lbuf, sjv, jjv, so, sp, scat, uto, uts, utp, ucat, gu, bs,
    tt, ol, nl, yl, zl_, yts, yf, gs, gx, gzl,
    in_s, out_s, s_loc, s_s, s_r, u_s, u_r, o_s, o_r, n_s, n_r, y_s, y_r, z_s, z_r,
    a_s, a_r, b_s, b_r, gx_s, gx_r, gz_s, gz_r, gb_s, gb_r, gd_s, gd_r,
):
    row = lax.axis_index("row")
    col = lax.axis_index("col")
    x, zh, k = row // 8, (row // 2) % 4, row % 2
    y, zl = col // 2, col % 2
    z = zh * 2 + zl
    other = 1 - k

    def dev(x, y, zh, zl, k):
        return ((x * 4 + zh) * 2 + k, y * 2 + zl)

    def at_x(d):
        return dev((x + d) % 4, y, zh, zl, k)

    def at_y(d):
        return dev(x, (y + d) % 4, zh, zl, k)

    def at_zh(d):
        return dev(x, y, (zh + d) % 4, zl, k)

    def at_z(d):
        t = (z + d) % 8
        return dev(x, y, t // 2, t % 2, k)

    partner = dev(x, y, zh, zl, other)
    cross = dev(x, y, zh, 1 - zl, other)
    peers = [partner, cross]
    peers += [at_z(d) for d in range(1, 8)]
    peers += [at_x(d) for d in (1, 2, 3)] + [at_y(d) for d in (1, 2, 3)]

    sent, outs = [], []

    def remote(src, dst, send, recv, device):
        return pltpu.make_async_remote_copy(
            src_ref=src, dst_ref=dst, send_sem=send, recv_sem=recv, device_id=device, device_id_type=MESH
        )

    def push(src, dst, send, recv, device):
        copy = remote(src, dst, send, recv, device)
        copy.start()
        sent.append(copy)

    def arrived(dst, send, recv):
        remote(dst, dst, send, recv, partner).wait_recv()

    barrier = pltpu.get_barrier_semaphore()
    for peer in peers:
        pl.semaphore_signal(barrier, inc=1, device_id=peer, device_id_type=MESH)

    loads = []
    for n, j in enumerate((other, k)):
        for m, (src, dst) in enumerate(((panel_ref, pbuf), (linv_ref, lbuf))):
            copy = pltpu.make_async_copy(src.at[j], dst.at[j], in_s.at[n, m])
            copy.start()
            loads.append(copy)

    offs = (2, 1, 3, 0)
    local = []
    for p in range(4):
        copy = pltpu.make_async_copy(s_ref.at[:, :, (x + offs[p]) % 4], so.at[p], s_loc.at[p])
        copy.start()
        local.append(copy)

    pattern = pattern_ref[...]
    for i in range(4):
        hit = jnp.where(pattern == i * 32 + row, 1.0, 0.0).astype(F32)
        for j in range(2):
            value = jnp.max(hit[j : j + 1], axis=1, keepdims=True)
            mask_ref[j, :, i * 128 : (i + 1) * 128] = jnp.broadcast_to(value, (8, 128))

    def update(j):
        a = split(pbuf[j])
        b = split(lbuf[j])
        return dot3(a, b).T * mask_ref[j, 0:1, :]

    loads[0].wait()
    loads[1].wait()
    uts[...] = update(other)
    pl.semaphore_wait(barrier, len(peers))
    for p in range(4):
        local[p].wait()
        push(so.at[p], sp.at[p], s_s.at[p], s_r.at[p], partner)
        if p == 0:
            push(uts, utp, u_s.at[0], u_r.at[0], partner)
    loads[2].wait()
    loads[3].wait()
    ut = update(k)
    uto[...] = ut
    ucat[:, 0:512], ucat[:, 1024:1536] = split(ut)

    def spread(p, half, src):
        def body(i, carry):
            r = pl.multiple_of(half * 512 + i * 128, 128)
            for m in range(4):
                hi, lo = split(src[p, i, m])
                scat[p, pl.ds(r, 128), m * 128 : (m + 1) * 128] = lo
                scat[p, pl.ds(1024 + r, 128), m * 128 : (m + 1) * 128] = hi
            return carry

        lax.fori_loop(0, 4, body, 0)

    def phase_p(p):
        spread(p, 0, so)
        if p == 0:
            arrived(utp, u_s.at[0], u_r.at[0])
            ucat[:, 512:1024], ucat[:, 1536:2048] = split(utp[...])
        arrived(sp.at[p], s_s.at[p], s_r.at[p])
        spread(p, 1, sp)
        dot = lambda a, b: jnp.dot(a, b, preferred_element_type=F32)
        tt[p] = dot(ucat[...], scat[p]) + dot(ucat[:, 0:1024], scat[p, 1024:2048])

    def phase_o(t):
        r = t * 128
        push(tt.at[0, r : r + 64], ol.at[t, 0], o_s.at[t, 0], o_r.at[t, 0], at_x(1))
        push(tt.at[0, r + 64 : r + 128], ol.at[t, 1], o_s.at[t, 1], o_r.at[t, 1], at_x(3))

    def phase_v(t):
        @pl.when(k == zl)
        def _():
            gu[0], gu[1] = split(uto[...].T)

        @pl.when(k != zl)
        def _():
            gu[0], gu[1] = split(utp[...].T)

        uto[...] = lbuf[k].T
        first = jnp.where((x == 0) & (z == 0), 1.0, 0.0).astype(F32)
        rows = [uto[pl.ds(pl.multiple_of(t * 128 + y * 32, 32), 32)] for t in range(CH)]
        base = dot3(split(jnp.concatenate(rows)), split(lbuf[k])) * first
        for t in range(CH):
            bs[t] = base[t * 32 : t * 32 + 32]

    def phase_b(t):
        for s in (0, 1):
            arrived(ol.at[t, s], o_s.at[t, s], o_r.at[t, s])
            r = slice(t * 128 + s * 64, t * 128 + s * 64 + 64)
            tt[1 + s, r] = tt[1 + s, r] + ol[t, s]
            push(tt.at[1 + s, t * 128 : t * 128 + 128], nl.at[t, s], n_s.at[t, s], n_r.at[t, s], at_x(1 + 2 * s))

    def phase_c(t):
        for s in (0, 1):
            arrived(nl.at[t, s], n_s.at[t, s], n_r.at[t, s])
        r = slice(t * 128, t * 128 + 128)
        tt[3, r] = tt[3, r] + (nl[t, 0] + nl[t, 1])
        for d in (1, 2, 3):
            q = (y + d) % 4
            push(tt.at[3, pl.ds(pl.multiple_of(t * 128 + q * 32, 32), 32)], yl.at[t, y], y_s.at[t, d], y_r.at[t, y], at_y(d))
        yl[t, y] = tt[3, pl.ds(pl.multiple_of(t * 128 + y * 32, 32), 32)]

    def phase_d(t):
        for d in (1, 2, 3):
            q = (y + d) % 4
            arrived(yl.at[t, q], y_s.at[t, d], y_r.at[t, q])
        for d in (1, 2, 3):
            q = (zh + d) % 4
            push(yl.at[t, q], zl_.at[t, zh], z_s.at[t, d], z_r.at[t, zh], at_zh(d))

    def phase_e(t):
        yt = yl[t, zh]
        for d in (1, 2, 3):
            q = (zh + d) % 4
            arrived(zl_.at[t, q], z_s.at[t, d], z_r.at[t, q])
            yt = yt + zl_[t, q]
        yts[t] = yt

        @pl.when(k == zl)
        def _():
            yf[t, y, k] = yt

        @pl.when(k != zl)
        def _():
            remote(yts.at[t], yf.at[t, y, k], a_s.at[t, 0], a_r.at[t, k], partner).start()

        push(yts.at[t], yf.at[t, y, k], a_s.at[t, 1], a_r.at[t, k], dev(x, y, zh, 1 - zl, zl))
        yh, yl_ = split(yt)
        b = t // 2
        c = slice(b * 256, 512)
        g = jnp.dot(jnp.concatenate([yh, yl_]), gu[0, :, c], preferred_element_type=F32)
        g2 = jnp.dot(yh, gu[1, :, c], preferred_element_type=F32)
        gs[t, :, c] = (g[0:32] + bs[t, :, c]) + (g[32:64] + g2)
        for d in (1, 2, 3) if t % 2 else ():
            r = pl.ds(pl.multiple_of((x + d) % 4 * 8, 8), 8)
            push(gs.at[t - 1 : t + 1, r, c], gx.at[b, x, :, :, c], gx_s.at[b, d], gx_r.at[b, x], at_x(d))

    def phase_f(t):
        arrived(yf.at[t, y, other], a_s.at[t, 0], a_r.at[t, other])

        @pl.when(k != zl)
        def _():
            arrived(yf.at[t, y, k], a_s.at[t, 0], a_r.at[t, k])

        for d in (1, 2, 3):
            push(yf.at[t, y], yf.at[t, y], b_s.at[t, d], b_r.at[t, y], at_y(d))
    def phase_m(b):
        t, c = slice(b * 2, b * 2 + 2), slice(b * 256, 512)
        g = gs[t, pl.ds(pl.multiple_of(x * 8, 8), 8), c]
        for d in (1, 2, 3):
            q = (x + d) % 4
            arrived(gx.at[b, q, :, :, c], gx_s.at[b, d], gx_r.at[b, q])
            g = g + gx[b, q, :, :, c]
        gzl[b, z, :, :, c] = g
        for d in range(1, 8):
            push(gzl.at[b, z, :, :, c], gzl.at[b, z, :, :, c], gz_s.at[b, d], gz_r.at[b, z], at_z(d))

    def piece(b, x, y):
        r = pl.ds(pl.multiple_of(y * 32 + x * 8, 8), 8)
        return jjv.at[k, b * 2 : b * 2 + 2, r, b * 256 : 512]

    def phase_g(b):
        t, c = slice(b * 2, b * 2 + 2), slice(b * 256, 512)
        for d in range(1, 8):
            q = (z + d) % 8
            arrived(gzl.at[b, q, :, :, c], gz_s.at[b, d], gz_r.at[b, q])
        g = gzl[b, 0, :, :, c]
        for q in range(1, 8):
            g = g + gzl[b, q, :, :, c]
        jjv[k, t, pl.ds(pl.multiple_of(y * 32 + x * 8, 8), 8), c] = g
        for d in (1, 2, 3):
            push(piece(b, x, y), piece(b, x, y), gb_s.at[b, d], gb_r.at[b, x * 4 + y], at_y(d))

    def phase_i(b):
        for dy in range(4):
            q = (y + dy) % 4
            part = piece(b, x, q)
            if dy:
                arrived(part, gb_s.at[b, dy], gb_r.at[b, x * 4 + q])
            for dx in (1, 2, 3):
                push(part, part, gb_s.at[b, dx * 4 + dy], gb_r.at[b, x * 4 + q], at_x(dx))

    def phase_h(b):
        for n in range(4, 16):
            dx, dy = n // 4, n % 4
            qx, qy = (x + dx) % 4, (y + dy) % 4
            arrived(piece(b, qx, qy), gb_s.at[b, n], gb_r.at[b, qx * 4 + qy])
        part = jjv.at[k, b * 2 : b * 2 + 2, :, b * 256 : 512]
        push(part, part, gd_s.at[b], gd_r.at[b], partner)

    def store(j, t, c, sem):
        copy = pltpu.make_async_copy(jjv.at[j, t, :, c], jj_ref.at[j, t, :, c], sem)
        copy.start()
        outs.append(copy)

    def phase_l(b):
        t, c = slice(b * 2, b * 2 + 2), slice(b * 256, 512)
        arrived(jjv.at[other, t, :, c], gd_s.at[b], gd_r.at[b])
        for j in range(2):
            store(j, t, c, out_s.at[b, 0, j])
            if b == 0:
                for n in (2, 3):
                    for m in (0, 1):
                        block = jjv[j, m, :, n * 128 : n * 128 + 128]
                        jjv[j, n, :, m * 128 : m * 128 + 128] = block.T
                store(j, slice(2, 4), slice(0, 256), out_s.at[b, 1, j])

    def phase_k(t):
        for d in (1, 2, 3):
            q = (y + d) % 4
            arrived(yf.at[t, q], b_s.at[t, d], b_r.at[t, q])
        for j in range(2):
            v = yf[t, :, j].reshape(128, 512) * (-mask_ref[j, 0:1, :])
            v = v.T
            for i in range(4):
                sjv[j, i, :, t * 128 : (t + 1) * 128] = v[i * 128 : (i + 1) * 128]
        c = slice(t * 128, t * 128 + 128)
        copy = pltpu.make_async_copy(sjv.at[:, :, :, c], sj_ref.at[:, :, :, c], out_s.at[t, 2, 0])
        copy.start()
        outs.append(copy)

    phases = dict(
        o=phase_o, p=phase_p, i=phase_i, v=phase_v, b=phase_b, c=phase_c, d=phase_d, e=phase_e, f=phase_f, g=phase_g,
        h=phase_h, k=phase_k, l=phase_l, m=phase_m,
    )
    for name, t in ORDER:
        phases[name](t)

    for copy in sent:
        copy.wait_send()
    for copy in outs:
        copy.wait()

    @pl.when(k != zl)
    def _():
        for t in range(CH):
            remote(yts.at[t], yf.at[t, y, k], a_s.at[t, 0], a_r.at[t, k], partner).wait_send()


def finish(sj_in, jj_in, sj_ref, jj_ref, sj_buf, jj_buf, in_s, out_s):
    parts = []
    for j in range(2):
        parts.append((sj_in.at[j], sj_buf.at[j], sj_ref.at[j], (0, j)))
        parts.append((jj_in.at[j], jj_buf.at[j], jj_ref.at[j], (1, j)))
    loads = [pltpu.make_async_copy(a, b, in_s.at[n]) for a, b, c, n in parts]
    stores = [pltpu.make_async_copy(b, c, out_s.at[n]) for a, b, c, n in parts]
    for copy in loads:
        copy.start()
    for load, store in zip(loads, stores):
        load.wait()
        store.start()
    for copy in stores:
        copy.wait()


def local(sigma_anc, panel, pattern, linv):
    s = sigma_anc.reshape(4, 4, 4, 128, 128)
    dma = pltpu.SemaphoreType.DMA
    vm = lambda *shape: pltpu.VMEM(shape, F32)
    vb = lambda *shape: pltpu.VMEM(shape, BF)
    pair = lambda *shape: [dma(shape), dma(shape)]
    results = pl.pallas_call(
        kernel,
        out_shape=(
            jax.ShapeDtypeStruct((2, 4, 128, 512), F32),
            jax.ShapeDtypeStruct((2, 4, 128, 512), F32),
        ),
        in_specs=[pl.BlockSpec(memory_space=pl.ANY)] * 3 + [pl.BlockSpec(memory_space=pltpu.VMEM)],
        out_specs=[pl.BlockSpec(memory_space=pl.ANY)] * 2,
        scratch_shapes=[
            vm(2, 8, 512), vm(2, 512, 512), vm(2, 512, 512), vm(2, 4, 128, 512), vm(2, 4, 128, 512),
            vm(4, 4, 4, 128, 128), vm(4, 4, 4, 128, 128),
            vb(4, 2048, 512), vm(512, 512), vm(512, 512), vm(512, 512), vb(512, 2048), vb(2, 512, 512),
            vm(CH, 32, 512), vm(4, 512, 512), vm(CH, 2, 64, 512), vm(CH, 2, 128, 512),
            vm(CH, 4, 32, 512), vm(CH, 4, 32, 512), vm(CH, 32, 512), vm(CH, 4, 2, 32, 512),
            vm(CH, 32, 512), vm(2, 4, 2, 8, 512), vm(2, 8, 2, 8, 512),
            dma((2, 2)), dma((CH, 3, 2)), dma((4,)), *pair(4), *pair(1), *pair(CH, 2), *pair(CH, 2), *pair(CH, 4), *pair(CH, 4),
            *pair(CH, 2), *pair(CH, 4), *pair(2, 4), *pair(2, 8), *pair(2, 16), *pair(2),
        ],
        compiler_params=pltpu.CompilerParams(
            collective_id=0, has_side_effects=True, vmem_limit_bytes=60 << 20
        ),
        name="selinv",
    )(s, panel.reshape(2, 512, 512), linv, pattern)
    sj, jj = pl.pallas_call(
        finish,
        out_shape=tuple(jax.ShapeDtypeStruct(v.shape, F32) for v in results),
        in_specs=[pl.BlockSpec(memory_space=pl.ANY)] * 2,
        out_specs=[pl.BlockSpec(memory_space=pl.ANY)] * 2,
        scratch_shapes=[vm(2, 4, 128, 512), vm(2, 4, 128, 512), dma((2, 2)), dma((2, 2))],
        name="finish",
    )(*results)
    return sj, jj.reshape(2, 512, 512)


def solution(mesh):
    return jax.shard_map(
        local,
        mesh=mesh,
        in_specs=(P("row", "col", None, None), P(None, "row", None, None), P(), P()),
        out_specs=(P(None, "row", None, None), P()),
        check_vma=False,
    )
```

```python
import jax
import jax.numpy as jnp
from jax import lax
from jax.experimental import pallas as pl
from jax.experimental.pallas import tpu as pltpu
from jax.sharding import PartitionSpec as P

MESH = pl.DeviceIdType.MESH
BF = jnp.bfloat16
F32 = jnp.float32
CH = 4
ORDER = (
    ("p", 0), ("o", 0), ("o", 1), ("o", 2), ("p", 1), ("p", 2), ("b", 0), ("o", 3),
    ("b", 1), ("p", 3), ("c", 0), ("b", 2), ("v", 0), ("b", 3), ("d", 0), ("c", 1),
    ("d", 1), ("c", 2), ("e", 0), ("d", 2), ("c", 3), ("f", 0), ("e", 1), ("d", 3),
    ("f", 1), ("e", 2), ("m", 0), ("m", 1), ("f", 2), ("e", 3), ("m", 2), ("g", 0),
    ("f", 3), ("m", 3), ("g", 1), ("g", 2), ("i", 0), ("k", 0), ("g", 3), ("i", 1),
    ("i", 2), ("k", 1), ("h", 0), ("i", 3), ("h", 1), ("l", 0), ("h", 2), ("k", 2),
    ("l", 1), ("h", 3), ("l", 2), ("k", 3), ("l", 3),
)
NN = (((1,), (0,)), ((), ()))


def split(v):
    hi = v.astype(BF)
    return hi, (v - hi.astype(F32)).astype(BF)


def dot3(a, b, dims=NN):
    dot = lambda p, q: lax.dot_general(p, q, dims, preferred_element_type=F32)
    return dot(a[0], b[0]) + (dot(a[0], b[1]) + dot(a[1], b[0]))


def kernel(
    s_ref, panel_ref, linv_ref, pattern_ref, sj_ref, jj_ref,
    mask_ref, pbuf, lbuf, sjv, jjv, so, sp, scat, uto, uts, utp, ucat, gu, bs,
    tt, ol, nl, yl, zl_, yts, yf, gs, gx, gzl,
    in_s, out_s, s_loc, s_s, s_r, u_s, u_r, o_s, o_r, n_s, n_r, y_s, y_r, z_s, z_r,
    a_s, a_r, b_s, b_r, gx_s, gx_r, gz_s, gz_r, gb_s, gb_r, gd_s, gd_r,
):
    row = lax.axis_index("row")
    col = lax.axis_index("col")
    x, zh, k = row // 8, (row // 2) % 4, row % 2
    y, zl = col // 2, col % 2
    z = zh * 2 + zl
    other = 1 - k

    def dev(x, y, zh, zl, k):
        return ((x * 4 + zh) * 2 + k, y * 2 + zl)

    def at_x(d):
        return dev((x + d) % 4, y, zh, zl, k)

    def at_y(d):
        return dev(x, (y + d) % 4, zh, zl, k)

    def at_zh(d):
        return dev(x, y, (zh + d) % 4, zl, k)

    def at_z(d):
        t = (z + d) % 8
        return dev(x, y, t // 2, t % 2, k)

    partner = dev(x, y, zh, zl, other)
    cross = dev(x, y, zh, 1 - zl, other)
    peers = [partner, cross]
    peers += [at_z(d) for d in range(1, 8)]
    peers += [at_x(d) for d in (1, 2, 3)] + [at_y(d) for d in (1, 2, 3)]

    sent, outs = [], []

    def remote(src, dst, send, recv, device):
        return pltpu.make_async_remote_copy(
            src_ref=src, dst_ref=dst, send_sem=send, recv_sem=recv, device_id=device, device_id_type=MESH
        )

    def push(src, dst, send, recv, device):
        copy = remote(src, dst, send, recv, device)
        copy.start()
        sent.append(copy)

    def arrived(dst, send, recv):
        remote(dst, dst, send, recv, partner).wait_recv()

    barrier = pltpu.get_barrier_semaphore()
    for peer in peers:
        pl.semaphore_signal(barrier, inc=1, device_id=peer, device_id_type=MESH)

    loads = []
    for n, j in enumerate((other, k)):
        for m, (src, dst) in enumerate(((panel_ref, pbuf), (linv_ref, lbuf))):
            copy = pltpu.make_async_copy(src.at[j], dst.at[j], in_s.at[n, m])
            copy.start()
            loads.append(copy)

    offs = (2, 1, 3, 0)
    local = []
    for p in range(4):
        copy = pltpu.make_async_copy(s_ref.at[:, :, (x + offs[p]) % 4], so.at[p], s_loc.at[p])
        copy.start()
        local.append(copy)

    pattern = pattern_ref[...]
    for i in range(4):
        hit = jnp.where(pattern == i * 32 + row, 1.0, 0.0).astype(F32)
        for j in range(2):
            value = jnp.max(hit[j : j + 1], axis=1, keepdims=True)
            mask_ref[j, :, i * 128 : (i + 1) * 128] = jnp.broadcast_to(value, (8, 128))

    def update(j):
        a = split(pbuf[j])
        b = split(lbuf[j])
        return dot3(a, b).T * mask_ref[j, 0:1, :]

    loads[0].wait()
    loads[1].wait()
    uts[...] = update(other)
    pl.semaphore_wait(barrier, len(peers))
    for p in range(4):
        local[p].wait()
        push(so.at[p], sp.at[p], s_s.at[p], s_r.at[p], partner)
        if p == 0:
            push(uts, utp, u_s.at[0], u_r.at[0], partner)
    loads[2].wait()
    loads[3].wait()
    ut = update(k)
    uto[...] = ut
    ucat[:, 0:512], ucat[:, 1024:1536] = split(ut)

    def spread(p, half, src):
        def body(i, carry):
            r = pl.multiple_of(half * 512 + i * 128, 128)
            for m in range(4):
                hi, lo = split(src[p, i, m])
                scat[p, pl.ds(r, 128), m * 128 : (m + 1) * 128] = lo
                scat[p, pl.ds(1024 + r, 128), m * 128 : (m + 1) * 128] = hi
            return carry

        lax.fori_loop(0, 4, body, 0)

    def phase_p(p):
        spread(p, 0, so)
        if p == 0:
            arrived(utp, u_s.at[0], u_r.at[0])
            ucat[:, 512:1024], ucat[:, 1536:2048] = split(utp[...])
        arrived(sp.at[p], s_s.at[p], s_r.at[p])
        spread(p, 1, sp)
        dot = lambda a, b: jnp.dot(a, b, preferred_element_type=F32)
        tt[p] = dot(ucat[...], scat[p]) + dot(ucat[:, 0:1024], scat[p, 1024:2048])

    def phase_o(t):
        r = t * 128
        push(tt.at[0, r : r + 64], ol.at[t, 0], o_s.at[t, 0], o_r.at[t, 0], at_x(1))
        push(tt.at[0, r + 64 : r + 128], ol.at[t, 1], o_s.at[t, 1], o_r.at[t, 1], at_x(3))

    def phase_v(t):
        @pl.when(k == zl)
        def _():
            gu[0], gu[1] = split(uto[...].T)

        @pl.when(k != zl)
        def _():
            gu[0], gu[1] = split(utp[...].T)

        uto[...] = lbuf[k].T
        first = jnp.where((x == 0) & (z == 0), 1.0, 0.0).astype(F32)
        rows = [uto[pl.ds(pl.multiple_of(t * 128 + y * 32, 32), 32)] for t in range(CH)]
        base = dot3(split(jnp.concatenate(rows)), split(lbuf[k])) * first
        for t in range(CH):
            bs[t] = base[t * 32 : t * 32 + 32]

    def phase_b(t):
        for s in (0, 1):
            arrived(ol.at[t, s], o_s.at[t, s], o_r.at[t, s])
            r = slice(t * 128 + s * 64, t * 128 + s * 64 + 64)
            tt[1 + s, r] = tt[1 + s, r] + ol[t, s]
            push(tt.at[1 + s, t * 128 : t * 128 + 128], nl.at[t, s], n_s.at[t, s], n_r.at[t, s], at_x(1 + 2 * s))

    def phase_c(t):
        for s in (0, 1):
            arrived(nl.at[t, s], n_s.at[t, s], n_r.at[t, s])
        r = slice(t * 128, t * 128 + 128)
        tt[3, r] = tt[3, r] + (nl[t, 0] + nl[t, 1])
        for d in (1, 2, 3):
            q = (y + d) % 4
            push(tt.at[3, pl.ds(pl.multiple_of(t * 128 + q * 32, 32), 32)], yl.at[t, y], y_s.at[t, d], y_r.at[t, y], at_y(d))
        yl[t, y] = tt[3, pl.ds(pl.multiple_of(t * 128 + y * 32, 32), 32)]

    def phase_d(t):
        for d in (1, 2, 3):
            q = (y + d) % 4
            arrived(yl.at[t, q], y_s.at[t, d], y_r.at[t, q])
        for d in (1, 2, 3):
            q = (zh + d) % 4
            push(yl.at[t, q], zl_.at[t, zh], z_s.at[t, d], z_r.at[t, zh], at_zh(d))

    def phase_e(t):
        yt = yl[t, zh]
        for d in (1, 2, 3):
            q = (zh + d) % 4
            arrived(zl_.at[t, q], z_s.at[t, d], z_r.at[t, q])
            yt = yt + zl_[t, q]
        yts[t] = yt

        @pl.when(k == zl)
        def _():
            yf[t, y, k] = yt

        @pl.when(k != zl)
        def _():
            remote(yts.at[t], yf.at[t, y, k], a_s.at[t, 0], a_r.at[t, k], partner).start()

        push(yts.at[t], yf.at[t, y, k], a_s.at[t, 1], a_r.at[t, k], dev(x, y, zh, 1 - zl, zl))
        yh, yl_ = split(yt)
        c = slice(t * 128, 512)
        g = jnp.dot(jnp.concatenate([yh, yl_]), gu[0, :, c], preferred_element_type=F32)
        g2 = jnp.dot(yh, gu[1, :, c], preferred_element_type=F32)
        gs[t, :, c] = (g[0:32] + bs[t, :, c]) + (g[32:64] + g2)
        for d in (1, 2, 3):
            r = pl.ds(pl.multiple_of((x + d) % 4 * 8, 8), 8)
            push(gs.at[t, r, c], gx.at[t, x, :, c], gx_s.at[t, d], gx_r.at[t, x], at_x(d))

    def phase_f(t):
        arrived(yf.at[t, y, other], a_s.at[t, 0], a_r.at[t, other])

        @pl.when(k != zl)
        def _():
            arrived(yf.at[t, y, k], a_s.at[t, 0], a_r.at[t, k])

        for d in (1, 2, 3):
            push(yf.at[t, y], yf.at[t, y], b_s.at[t, d], b_r.at[t, y], at_y(d))
    def phase_m(t):
        c = slice(t * 128, 512)
        g = gs[t, pl.ds(pl.multiple_of(x * 8, 8), 8), c]
        for d in (1, 2, 3):
            q = (x + d) % 4
            arrived(gx.at[t, q, :, c], gx_s.at[t, d], gx_r.at[t, q])
            g = g + gx[t, q, :, c]
        gzl[t, z, :, c] = g
        for d in range(1, 8):
            push(gzl.at[t, z, :, c], gzl.at[t, z, :, c], gz_s.at[t, d], gz_r.at[t, z], at_z(d))

    def tile_row(t, x, y):
        return pl.ds(pl.multiple_of(t * 128 + y * 32 + x * 8, 8), 8)

    def phase_g(t):
        c = slice(t * 128, 512)
        for d in range(1, 8):
            q = (z + d) % 8
            arrived(gzl.at[t, q, :, c], gz_s.at[t, d], gz_r.at[t, q])
        g = gzl[t, 0, :, c]
        for q in range(1, 8):
            g = g + gzl[t, q, :, c]
        r = tile_row(t, x, y)
        jjv[k, r, c] = g
        for d in (1, 2, 3):
            push(jjv.at[k, r, c], jjv.at[k, r, c], gb_s.at[t, d], gb_r.at[t, x * 4 + y], at_y(d))

    def phase_i(t):
        c = slice(t * 128, 512)
        for dy in range(4):
            q = (y + dy) % 4
            r = tile_row(t, x, q)
            if dy:
                arrived(jjv.at[k, r, c], gb_s.at[t, dy], gb_r.at[t, x * 4 + q])
            for dx in (1, 2, 3):
                push(jjv.at[k, r, c], jjv.at[k, r, c], gb_s.at[t, dx * 4 + dy], gb_r.at[t, x * 4 + q], at_x(dx))

    def store(t, j, side):
        r, c = slice(t * 128, t * 128 + 128), slice(t * 128, 512)
        if side:
            r, c = slice(t * 128 + 128, 512), r
        copy = pltpu.make_async_copy(jjv.at[j, r, c], jj_ref.at[j, r, c], out_s.at[t, side, j])
        copy.start()
        outs.append(copy)

    def mirror(t, j):
        r = slice(t * 128, t * 128 + 128)
        for n in range(t + 1, 4):
            c = slice(n * 128, n * 128 + 128)
            jjv[j, c, r] = jjv[j, r, c].T

    def phase_h(t):
        r, c = slice(t * 128, t * 128 + 128), slice(t * 128, 512)
        for n in range(4, 16):
            dx, dy = n // 4, n % 4
            qx, qy = (x + dx) % 4, (y + dy) % 4
            arrived(jjv.at[k, tile_row(t, qx, qy), c], gb_s.at[t, n], gb_r.at[t, qx * 4 + qy])
        push(jjv.at[k, r, c], jjv.at[k, r, c], gd_s.at[t], gd_r.at[t], partner)

    def phase_k(t):
        for d in (1, 2, 3):
            q = (y + d) % 4
            arrived(yf.at[t, q], b_s.at[t, d], b_r.at[t, q])
        for j in range(2):
            v = yf[t, :, j].reshape(128, 512) * (-mask_ref[j, 0:1, :])
            v = v.T
            for i in range(4):
                sjv[j, i, :, t * 128 : (t + 1) * 128] = v[i * 128 : (i + 1) * 128]
        c = slice(t * 128, t * 128 + 128)
        copy = pltpu.make_async_copy(sjv.at[:, :, :, c], sj_ref.at[:, :, :, c], out_s.at[t, 2, 0])
        copy.start()
        outs.append(copy)

    def phase_l(t):
        r, c = slice(t * 128, t * 128 + 128), slice(t * 128, 512)
        arrived(jjv.at[other, r, c], gd_s.at[t], gd_r.at[t])
        for j in range(2):
            store(t, j, 0)
            if t < 3:
                mirror(t, j)
                store(t, j, 1)

    phases = dict(
        o=phase_o, p=phase_p, i=phase_i, v=phase_v, b=phase_b, c=phase_c, d=phase_d, e=phase_e, f=phase_f, g=phase_g,
        h=phase_h, k=phase_k, l=phase_l, m=phase_m,
    )
    for name, t in ORDER:
        phases[name](t)

    for copy in sent:
        copy.wait_send()
    for copy in outs:
        copy.wait()

    @pl.when(k != zl)
    def _():
        for t in range(CH):
            remote(yts.at[t], yf.at[t, y, k], a_s.at[t, 0], a_r.at[t, k], partner).wait_send()


def finish(sj_in, jj_in, sj_ref, jj_ref, sj_buf, jj_buf, in_s, out_s):
    parts = []
    for j in range(2):
        parts.append((sj_in.at[j], sj_buf.at[j], sj_ref.at[j], (0, j)))
        parts.append((jj_in.at[j], jj_buf.at[j], jj_ref.at[j], (1, j)))
    loads = [pltpu.make_async_copy(a, b, in_s.at[n]) for a, b, c, n in parts]
    stores = [pltpu.make_async_copy(b, c, out_s.at[n]) for a, b, c, n in parts]
    for copy in loads:
        copy.start()
    for load, store in zip(loads, stores):
        load.wait()
        store.start()
    for copy in stores:
        copy.wait()


def local(sigma_anc, panel, pattern, linv):
    s = sigma_anc.reshape(4, 4, 4, 128, 128)
    dma = pltpu.SemaphoreType.DMA
    vm = lambda *shape: pltpu.VMEM(shape, F32)
    vb = lambda *shape: pltpu.VMEM(shape, BF)
    pair = lambda *shape: [dma(shape), dma(shape)]
    results = pl.pallas_call(
        kernel,
        out_shape=(
            jax.ShapeDtypeStruct((2, 4, 128, 512), F32),
            jax.ShapeDtypeStruct((2, 512, 512), F32),
        ),
        in_specs=[pl.BlockSpec(memory_space=pl.ANY)] * 3 + [pl.BlockSpec(memory_space=pltpu.VMEM)],
        out_specs=[pl.BlockSpec(memory_space=pl.ANY)] * 2,
        scratch_shapes=[
            vm(2, 8, 512), vm(2, 512, 512), vm(2, 512, 512), vm(2, 4, 128, 512), vm(2, 512, 512),
            vm(4, 4, 4, 128, 128), vm(4, 4, 4, 128, 128),
            vb(4, 2048, 512), vm(512, 512), vm(512, 512), vm(512, 512), vb(512, 2048), vb(2, 512, 512),
            vm(CH, 32, 512), vm(4, 512, 512), vm(CH, 2, 64, 512), vm(CH, 2, 128, 512),
            vm(CH, 4, 32, 512), vm(CH, 4, 32, 512), vm(CH, 32, 512), vm(CH, 4, 2, 32, 512),
            vm(CH, 32, 512), vm(CH, 4, 8, 512), vm(CH, 8, 8, 512),
            dma((2, 2)), dma((CH, 3, 2)), dma((4,)), *pair(4), *pair(1), *pair(CH, 2), *pair(CH, 2), *pair(CH, 4), *pair(CH, 4),
            *pair(CH, 2), *pair(CH, 4), *pair(CH, 4), *pair(CH, 8), *pair(CH, 16), *pair(CH),
        ],
        compiler_params=pltpu.CompilerParams(
            collective_id=0, has_side_effects=True, vmem_limit_bytes=60 << 20
        ),
        name="selinv",
    )(s, panel.reshape(2, 512, 512), linv, pattern)
    return pl.pallas_call(
        finish,
        out_shape=tuple(jax.ShapeDtypeStruct(v.shape, F32) for v in results),
        in_specs=[pl.BlockSpec(memory_space=pl.ANY)] * 2,
        out_specs=[pl.BlockSpec(memory_space=pl.ANY)] * 2,
        scratch_shapes=[vm(2, 4, 128, 512), vm(2, 512, 512), dma((2, 2)), dma((2, 2))],
        name="finish",
    )(*results)


def solution(mesh):
    return jax.shard_map(
        local,
        mesh=mesh,
        in_specs=(P("row", "col", None, None), P(None, "row", None, None), P(), P()),
        out_specs=(P(None, "row", None, None), P()),
        check_vma=False,
    )
```

```python
import jax
import jax.numpy as jnp
from jax import lax
from jax.experimental import pallas as pl
from jax.experimental.pallas import tpu as pltpu
from jax.sharding import PartitionSpec as P

MESH = pl.DeviceIdType.MESH
BF = jnp.bfloat16
F32 = jnp.float32
CH = 4
ORDER = (
    ("p", 0), ("o", 0), ("o", 1), ("o", 2), ("p", 1), ("p", 2), ("b", 0), ("o", 3),
    ("b", 1), ("p", 3), ("c", 0), ("b", 2), ("v", 0), ("b", 3), ("d", 0), ("c", 1),
    ("d", 1), ("c", 2), ("e", 0), ("d", 2), ("c", 3), ("f", 0), ("e", 1), ("d", 3),
    ("f", 1), ("e", 2), ("m", 0), ("m", 1), ("f", 2), ("e", 3), ("m", 2), ("g", 0),
    ("f", 3), ("m", 3), ("g", 1), ("g", 2), ("i", 0), ("k", 0), ("g", 3), ("i", 1),
    ("i", 2), ("k", 1), ("h", 0), ("i", 3), ("h", 1), ("l", 0), ("h", 2), ("k", 2),
    ("l", 1), ("h", 3), ("l", 2), ("k", 3), ("l", 3),
)
NN = (((1,), (0,)), ((), ()))


def split(v):
    hi = v.astype(BF)
    return hi, (v - hi.astype(F32)).astype(BF)


def dot3(a, b, dims=NN):
    dot = lambda p, q: lax.dot_general(p, q, dims, preferred_element_type=F32)
    return dot(a[0], b[0]) + (dot(a[0], b[1]) + dot(a[1], b[0]))


def kernel(
    s_ref, panel_ref, linv_ref, pattern_ref, sj_ref, jj_ref,
    mask_ref, pbuf, lbuf, sjv, jjv, so, sp, scat, uto, uts, utp, ucat, gu, bs,
    tt, ol, nl, yl, zl_, yts, yf, gs, gx, gzl,
    in_s, out_s, s_loc, s_s, s_r, u_s, u_r, o_s, o_r, n_s, n_r, y_s, y_r, z_s, z_r,
    a_s, a_r, b_s, b_r, gx_s, gx_r, gz_s, gz_r, gb_s, gb_r, gd_s, gd_r,
):
    row = lax.axis_index("row")
    col = lax.axis_index("col")
    x, zh, k = row // 8, (row // 2) % 4, row % 2
    y, zl = col // 2, col % 2
    z = zh * 2 + zl
    other = 1 - k

    def dev(x, y, zh, zl, k):
        return ((x * 4 + zh) * 2 + k, y * 2 + zl)

    def at_x(d):
        return dev((x + d) % 4, y, zh, zl, k)

    def at_y(d):
        return dev(x, (y + d) % 4, zh, zl, k)

    def at_zh(d):
        return dev(x, y, (zh + d) % 4, zl, k)

    def at_z(d):
        t = (z + d) % 8
        return dev(x, y, t // 2, t % 2, k)

    partner = dev(x, y, zh, zl, other)
    cross = dev(x, y, zh, 1 - zl, other)
    peers = [partner, cross]
    peers += [at_z(d) for d in range(1, 8)]
    peers += [at_x(d) for d in (1, 2, 3)] + [at_y(d) for d in (1, 2, 3)]

    sent, outs = [], []

    def remote(src, dst, send, recv, device):
        return pltpu.make_async_remote_copy(
            src_ref=src, dst_ref=dst, send_sem=send, recv_sem=recv, device_id=device, device_id_type=MESH
        )

    def push(src, dst, send, recv, device):
        copy = remote(src, dst, send, recv, device)
        copy.start()
        sent.append(copy)

    def arrived(dst, send, recv):
        remote(dst, dst, send, recv, partner).wait_recv()

    barrier = pltpu.get_barrier_semaphore()
    for peer in peers:
        pl.semaphore_signal(barrier, inc=1, device_id=peer, device_id_type=MESH)

    offs = (2, 1, 3, 0)
    local = []
    for p in range(4):
        copy = pltpu.make_async_copy(s_ref.at[:, :, (x + offs[p]) % 4], so.at[p], s_loc.at[p])
        copy.start()
        local.append(copy)

    loads = []
    for n, j in enumerate((other, k)):
        for m, (src, dst) in enumerate(((panel_ref, pbuf), (linv_ref, lbuf))):
            copy = pltpu.make_async_copy(src.at[j], dst.at[j], in_s.at[n, m])
            copy.start()
            loads.append(copy)

    pattern = pattern_ref[...]
    for i in range(4):
        hit = jnp.where(pattern == i * 32 + row, 1.0, 0.0).astype(F32)
        for j in range(2):
            value = jnp.max(hit[j : j + 1], axis=1, keepdims=True)
            mask_ref[j, :, i * 128 : (i + 1) * 128] = jnp.broadcast_to(value, (8, 128))

    def update(j):
        a = split(pbuf[j])
        b = split(lbuf[j])
        return dot3(a, b).T * mask_ref[j, 0:1, :]

    loads[0].wait()
    loads[1].wait()
    uts[...] = update(other)
    pl.semaphore_wait(barrier, len(peers))
    for p in range(4):
        local[p].wait()
        push(so.at[p], sp.at[p], s_s.at[p], s_r.at[p], partner)
        if p == 0:
            push(uts, utp, u_s.at[0], u_r.at[0], partner)
    loads[2].wait()
    loads[3].wait()
    ut = update(k)
    uto[...] = ut
    ucat[:, 0:512], ucat[:, 1024:1536] = split(ut)

    def spread(p, half, src):
        def body(i, carry):
            r = pl.multiple_of(half * 512 + i * 128, 128)
            for m in range(4):
                hi, lo = split(src[p, i, m])
                scat[p, pl.ds(r, 128), m * 128 : (m + 1) * 128] = lo
                scat[p, pl.ds(1024 + r, 128), m * 128 : (m + 1) * 128] = hi
            return carry

        lax.fori_loop(0, 4, body, 0)

    def phase_p(p):
        spread(p, 0, so)
        if p == 0:
            arrived(utp, u_s.at[0], u_r.at[0])
            ucat[:, 512:1024], ucat[:, 1536:2048] = split(utp[...])
        arrived(sp.at[p], s_s.at[p], s_r.at[p])
        spread(p, 1, sp)
        dot = lambda a, b: jnp.dot(a, b, preferred_element_type=F32)
        tt[p] = dot(ucat[...], scat[p]) + dot(ucat[:, 0:1024], scat[p, 1024:2048])

    def phase_o(t):
        r = t * 128
        push(tt.at[0, r : r + 64], ol.at[t, 0], o_s.at[t, 0], o_r.at[t, 0], at_x(1))
        push(tt.at[0, r + 64 : r + 128], ol.at[t, 1], o_s.at[t, 1], o_r.at[t, 1], at_x(3))

    def phase_v(t):
        @pl.when(k == zl)
        def _():
            gu[0], gu[1] = split(uto[...].T)

        @pl.when(k != zl)
        def _():
            gu[0], gu[1] = split(utp[...].T)

        uto[...] = lbuf[k].T
        first = jnp.where((x == 0) & (z == 0), 1.0, 0.0).astype(F32)
        rows = [uto[pl.ds(pl.multiple_of(t * 128 + y * 32, 32), 32)] for t in range(CH)]
        base = dot3(split(jnp.concatenate(rows)), split(lbuf[k])) * first
        for t in range(CH):
            bs[t] = base[t * 32 : t * 32 + 32]

    def phase_b(t):
        for s in (0, 1):
            arrived(ol.at[t, s], o_s.at[t, s], o_r.at[t, s])
            r = slice(t * 128 + s * 64, t * 128 + s * 64 + 64)
            tt[1 + s, r] = tt[1 + s, r] + ol[t, s]
            push(tt.at[1 + s, t * 128 : t * 128 + 128], nl.at[t, s], n_s.at[t, s], n_r.at[t, s], at_x(1 + 2 * s))

    def phase_c(t):
        for s in (0, 1):
            arrived(nl.at[t, s], n_s.at[t, s], n_r.at[t, s])
        r = slice(t * 128, t * 128 + 128)
        tt[3, r] = tt[3, r] + (nl[t, 0] + nl[t, 1])
        for d in (1, 2, 3):
            q = (y + d) % 4
            push(tt.at[3, pl.ds(pl.multiple_of(t * 128 + q * 32, 32), 32)], yl.at[t, y], y_s.at[t, d], y_r.at[t, y], at_y(d))
        yl[t, y] = tt[3, pl.ds(pl.multiple_of(t * 128 + y * 32, 32), 32)]

    def phase_d(t):
        for d in (1, 2, 3):
            q = (y + d) % 4
            arrived(yl.at[t, q], y_s.at[t, d], y_r.at[t, q])
        for d in (1, 2, 3):
            q = (zh + d) % 4
            push(yl.at[t, q], zl_.at[t, zh], z_s.at[t, d], z_r.at[t, zh], at_zh(d))

    def phase_e(t):
        yt = yl[t, zh]
        for d in (1, 2, 3):
            q = (zh + d) % 4
            arrived(zl_.at[t, q], z_s.at[t, d], z_r.at[t, q])
            yt = yt + zl_[t, q]
        yts[t] = yt

        @pl.when(k == zl)
        def _():
            yf[t, y, k] = yt

        @pl.when(k != zl)
        def _():
            remote(yts.at[t], yf.at[t, y, k], a_s.at[t, 0], a_r.at[t, k], partner).start()

        push(yts.at[t], yf.at[t, y, k], a_s.at[t, 1], a_r.at[t, k], dev(x, y, zh, 1 - zl, zl))
        yh, yl_ = split(yt)
        c = slice(t * 128, 512)
        g = jnp.dot(jnp.concatenate([yh, yl_]), gu[0, :, c], preferred_element_type=F32)
        g2 = jnp.dot(yh, gu[1, :, c], preferred_element_type=F32)
        gs[t, :, c] = (g[0:32] + bs[t, :, c]) + (g[32:64] + g2)
        for d in (1, 2, 3):
            r = pl.ds(pl.multiple_of((x + d) % 4 * 8, 8), 8)
            push(gs.at[t, r, c], gx.at[t, x, :, c], gx_s.at[t, d], gx_r.at[t, x], at_x(d))

    def phase_f(t):
        arrived(yf.at[t, y, other], a_s.at[t, 0], a_r.at[t, other])

        @pl.when(k != zl)
        def _():
            arrived(yf.at[t, y, k], a_s.at[t, 0], a_r.at[t, k])

        for d in (1, 2, 3):
            push(yf.at[t, y], yf.at[t, y], b_s.at[t, d], b_r.at[t, y], at_y(d))
    def phase_m(t):
        c = slice(t * 128, 512)
        g = gs[t, pl.ds(pl.multiple_of(x * 8, 8), 8), c]
        for d in (1, 2, 3):
            q = (x + d) % 4
            arrived(gx.at[t, q, :, c], gx_s.at[t, d], gx_r.at[t, q])
            g = g + gx[t, q, :, c]
        gzl[t, z, :, c] = g
        for d in range(1, 8):
            push(gzl.at[t, z, :, c], gzl.at[t, z, :, c], gz_s.at[t, d], gz_r.at[t, z], at_z(d))

    def tile_row(t, x, y):
        return pl.ds(pl.multiple_of(t * 128 + y * 32 + x * 8, 8), 8)

    def phase_g(t):
        c = slice(t * 128, 512)
        for d in range(1, 8):
            q = (z + d) % 8
            arrived(gzl.at[t, q, :, c], gz_s.at[t, d], gz_r.at[t, q])
        g = gzl[t, 0, :, c]
        for q in range(1, 8):
            g = g + gzl[t, q, :, c]
        r = tile_row(t, x, y)
        jjv[k, r, c] = g
        for d in (1, 2, 3):
            push(jjv.at[k, r, c], jjv.at[k, r, c], gb_s.at[t, d], gb_r.at[t, x * 4 + y], at_y(d))

    def phase_i(t):
        c = slice(t * 128, 512)
        for dy in range(4):
            q = (y + dy) % 4
            r = tile_row(t, x, q)
            if dy:
                arrived(jjv.at[k, r, c], gb_s.at[t, dy], gb_r.at[t, x * 4 + q])
            for dx in (1, 2, 3):
                push(jjv.at[k, r, c], jjv.at[k, r, c], gb_s.at[t, dx * 4 + dy], gb_r.at[t, x * 4 + q], at_x(dx))

    def store(t, j, side):
        r, c = slice(t * 128, t * 128 + 128), slice(t * 128, 512)
        if side:
            r, c = slice(t * 128 + 128, 512), r
        copy = pltpu.make_async_copy(jjv.at[j, r, c], jj_ref.at[j, r, c], out_s.at[t, side, j])
        copy.start()
        outs.append(copy)

    def mirror(t, j):
        r = slice(t * 128, t * 128 + 128)
        for n in range(t + 1, 4):
            c = slice(n * 128, n * 128 + 128)
            jjv[j, c, r] = jjv[j, r, c].T

    def phase_h(t):
        r, c = slice(t * 128, t * 128 + 128), slice(t * 128, 512)
        for n in range(4, 16):
            dx, dy = n // 4, n % 4
            qx, qy = (x + dx) % 4, (y + dy) % 4
            arrived(jjv.at[k, tile_row(t, qx, qy), c], gb_s.at[t, n], gb_r.at[t, qx * 4 + qy])
        push(jjv.at[k, r, c], jjv.at[k, r, c], gd_s.at[t], gd_r.at[t], partner)

    def phase_k(t):
        for d in (1, 2, 3):
            q = (y + d) % 4
            arrived(yf.at[t, q], b_s.at[t, d], b_r.at[t, q])
        for j in range(2):
            v = yf[t, :, j].reshape(128, 512) * (-mask_ref[j, 0:1, :])
            v = v.T
            for i in range(4):
                sjv[j, i, :, t * 128 : (t + 1) * 128] = v[i * 128 : (i + 1) * 128]
        c = slice(t * 128, t * 128 + 128)
        copy = pltpu.make_async_copy(sjv.at[:, :, :, c], sj_ref.at[:, :, :, c], out_s.at[t, 2, 0])
        copy.start()
        outs.append(copy)

    def phase_l(t):
        r, c = slice(t * 128, t * 128 + 128), slice(t * 128, 512)
        arrived(jjv.at[other, r, c], gd_s.at[t], gd_r.at[t])
        for j in range(2):
            store(t, j, 0)
            if t < 3:
                mirror(t, j)
                store(t, j, 1)

    phases = dict(
        o=phase_o, p=phase_p, i=phase_i, v=phase_v, b=phase_b, c=phase_c, d=phase_d, e=phase_e, f=phase_f, g=phase_g,
        h=phase_h, k=phase_k, l=phase_l, m=phase_m,
    )
    for name, t in ORDER:
        phases[name](t)

    for copy in sent:
        copy.wait_send()
    for copy in outs:
        copy.wait()

    @pl.when(k != zl)
    def _():
        for t in range(CH):
            remote(yts.at[t], yf.at[t, y, k], a_s.at[t, 0], a_r.at[t, k], partner).wait_send()


def finish(sj_in, jj_in, sj_ref, jj_ref, sj_buf, jj_buf, in_s, out_s):
    parts = []
    for j in range(2):
        parts.append((sj_in.at[j], sj_buf.at[j], sj_ref.at[j], (0, j)))
        parts.append((jj_in.at[j], jj_buf.at[j], jj_ref.at[j], (1, j)))
    loads = [pltpu.make_async_copy(a, b, in_s.at[n]) for a, b, c, n in parts]
    stores = [pltpu.make_async_copy(b, c, out_s.at[n]) for a, b, c, n in parts]
    for copy in loads:
        copy.start()
    for load, store in zip(loads, stores):
        load.wait()
        store.start()
    for copy in stores:
        copy.wait()


def local(sigma_anc, panel, pattern, linv):
    s = sigma_anc.reshape(4, 4, 4, 128, 128)
    dma = pltpu.SemaphoreType.DMA
    vm = lambda *shape: pltpu.VMEM(shape, F32)
    vb = lambda *shape: pltpu.VMEM(shape, BF)
    pair = lambda *shape: [dma(shape), dma(shape)]
    results = pl.pallas_call(
        kernel,
        out_shape=(
            jax.ShapeDtypeStruct((2, 4, 128, 512), F32),
            jax.ShapeDtypeStruct((2, 512, 512), F32),
        ),
        in_specs=[pl.BlockSpec(memory_space=pl.ANY)] * 3 + [pl.BlockSpec(memory_space=pltpu.VMEM)],
        out_specs=[pl.BlockSpec(memory_space=pl.ANY)] * 2,
        scratch_shapes=[
            vm(2, 8, 512), vm(2, 512, 512), vm(2, 512, 512), vm(2, 4, 128, 512), vm(2, 512, 512),
            vm(4, 4, 4, 128, 128), vm(4, 4, 4, 128, 128),
            vb(4, 2048, 512), vm(512, 512), vm(512, 512), vm(512, 512), vb(512, 2048), vb(2, 512, 512),
            vm(CH, 32, 512), vm(4, 512, 512), vm(CH, 2, 64, 512), vm(CH, 2, 128, 512),
            vm(CH, 4, 32, 512), vm(CH, 4, 32, 512), vm(CH, 32, 512), vm(CH, 4, 2, 32, 512),
            vm(CH, 32, 512), vm(CH, 4, 8, 512), vm(CH, 8, 8, 512),
            dma((2, 2)), dma((CH, 3, 2)), dma((4,)), *pair(4), *pair(1), *pair(CH, 2), *pair(CH, 2), *pair(CH, 4), *pair(CH, 4),
            *pair(CH, 2), *pair(CH, 4), *pair(CH, 4), *pair(CH, 8), *pair(CH, 16), *pair(CH),
        ],
        compiler_params=pltpu.CompilerParams(
            collective_id=0, has_side_effects=True, vmem_limit_bytes=60 << 20
        ),
        name="selinv",
    )(s, panel.reshape(2, 512, 512), linv, pattern)
    return pl.pallas_call(
        finish,
        out_shape=tuple(jax.ShapeDtypeStruct(v.shape, F32) for v in results),
        in_specs=[pl.BlockSpec(memory_space=pl.ANY)] * 2,
        out_specs=[pl.BlockSpec(memory_space=pl.ANY)] * 2,
        scratch_shapes=[vm(2, 4, 128, 512), vm(2, 512, 512), dma((2, 2)), dma((2, 2))],
        name="finish",
    )(*results)


def solution(mesh):
    return jax.shard_map(
        local,
        mesh=mesh,
        in_specs=(P("row", "col", None, None), P(None, "row", None, None), P(), P()),
        out_specs=(P(None, "row", None, None), P()),
        check_vma=False,
    )
```
